256 devices in a mesh: date: 32 (over x, y, core), tile: 8 (over z).
Axes of the slice: x: 4, y: 4, z: 8, core: 2. Of those that a mesh axis runs over, the one named last changes fastest.
Arguments:
- slc: bfloat16 [2, 256, 10, 20480], P(None, 'date', None, 'tile'), may hold values from -3 to 3
- offsets: int32 [256, 20], replicated, may hold values from 0 to 24, as said below
Outputs:
- series: float32 [256, 8, 256], P(None, 'tile', 'date')
The draws below stay inside these ranges and needn't reach their ends.
Inputs may be any that keep to these rules, and one draw needn't show every extreme that they name: In row d the live entries come first, are distinct, and satisfy d + offsets[d, k] <= 255; row d has min(c, 255 - d, 24) live entries with c from 4 to 20; the 8 rows of one index of date hold at most 100 live entries together, exactly 100 on some index; the remaining entries are 0.
All inputs are finite; a program needn't handle non-finite values.
Results may differ from the reference program's by a relative error of at most 0.0003.
Values may be sent and summed in bfloat16 or wider, within the bound.
A program may use at most 64 MiB of HBM per device.

```python
import math
from functools import partial
import jax
import jax.numpy as jnp
from jax import lax

DATE_DEV = 8
DATES = 256
ROWS = 10
COLS = 20480
LOOK_AZ = 5
LOOK_RG = 20
MAXP = 20
SPAN = 24
ITERS = 2
N_DATE = 32
N_TILE = 8


def draw_offsets(key, part):
    date_count = DATES
    date_local = DATE_DEV
    device_count = date_count // date_local
    subkeys = jax.random.split(jax.random.fold_in(key, 11), 5)
    pattern = jax.random.randint(subkeys[0], (device_count,), 0, 8)
    table = jnp.array([0, 0, 0, 0, 1, 1, 2, 4], jnp.int32)
    busy_number = table[pattern]
    forced = jax.random.randint(subkeys[1], (), 0, device_count - 3)
    is_forced = jnp.arange(device_count, dtype=jnp.int32) == forced
    busy_number = jnp.where(is_forced, 4, busy_number)
    date_scores = jax.random.randint(subkeys[2], (device_count, date_local), 0, 2 ** 20) * 16 + jnp.arange(date_local, dtype=jnp.int32)[None, :]
    date_rank = jnp.argsort(jnp.argsort(date_scores, axis=1, stable=True), axis=1, stable=True)
    is_busy = date_rank < busy_number[:, None]
    quiet = jax.random.randint(subkeys[3], (device_count, date_local), 4, 6)
    quiet = jnp.where(is_forced[:, None], 5, quiet)
    wanted = jnp.where(is_busy, MAXP, quiet).reshape(date_count)
    row_ids = jnp.arange(date_count, dtype=jnp.int32)
    available = jnp.minimum(SPAN, date_count - 1 - row_ids)
    having = jnp.minimum(wanted, available)
    distances = jnp.arange(1, SPAN + 1, dtype=jnp.int32)
    spread = jax.random.randint(subkeys[4], (date_count, SPAN), 0, 2 ** 10)
    scores = spread * (distances * distances)[None, :] * 32 + distances[None, :]
    usable = row_ids[:, None] + distances[None, :] <= date_count - 1
    scores = jnp.where(usable, scores, scores + 2 ** 26)
    first_row = forced * date_local
    scores = jnp.where((row_ids[:, None] == first_row) & (distances[None, :] == SPAN), -1, scores)
    order = jnp.argsort(scores, axis=1, stable=True)
    sorted_distances = jnp.take_along_axis(jnp.broadcast_to(distances[None, :], (date_count, SPAN)), order, axis=1)
    leading = sorted_distances[:, :MAXP]
    keep = jnp.arange(MAXP, dtype=jnp.int32)[None, :] < having[:, None]
    return jnp.where(keep, leading, 0).astype(jnp.int32)


def draw_slc(key, part):
    date_count = DATES
    height = ROWS
    total_width = COLS
    look_rows = height // LOOK_AZ
    look_cols = total_width // LOOK_RG
    subkeys = jax.random.split(jax.random.fold_in(key, 23), 6)
    speckle = jax.random.uniform(subkeys[0], (height, total_width), jnp.float32, -math.pi, math.pi)
    coherence_pick = jax.random.randint(subkeys[5], (look_rows, look_cols), 0, 2)
    amplitude = jax.random.uniform(subkeys[1], (date_count, height, total_width), jnp.float32, 0.3, 1.7)
    sample_noise = jax.random.uniform(subkeys[2], (date_count, height, total_width), jnp.float32, -0.3, 0.3)
    coarse_noise = jax.random.uniform(subkeys[3], (date_count, look_rows, look_cols), jnp.float32, -0.2, 0.2)
    drift = jax.random.uniform(subkeys[4], (look_rows, look_cols), jnp.float32, 0.004, 0.02)
    coherence = jnp.where(coherence_pick == 1, 2.0, 0.1).astype(jnp.float32)
    coherence_full = jnp.repeat(jnp.repeat(coherence, LOOK_AZ, axis=0), LOOK_RG, axis=1)
    sample_noise = sample_noise * coherence_full[None]
    coarse_noise = coarse_noise * coherence[None]
    coarse_full = jnp.repeat(jnp.repeat(coarse_noise, LOOK_AZ, axis=1), LOOK_RG, axis=2)
    drift_full = jnp.repeat(jnp.repeat(drift, LOOK_AZ, axis=0), LOOK_RG, axis=1)
    date_steps = jnp.arange(date_count, dtype=jnp.float32)[:, None, None]
    angle_field = speckle[None] + sample_noise + coarse_full + drift_full[None] * date_steps
    return jnp.stack([amplitude * jnp.cos(angle_field), amplitude * jnp.sin(angle_field)]).astype(jnp.bfloat16)


def setup_inputs(seed: int = 0) -> dict:
    key_list = jax.random.split(jax.random.key(seed), 3)
    return {
        "slc": draw_slc(jax.random.fold_in(key_list[2], 71), 0),
        "offsets": draw_offsets(jax.random.fold_in(key_list[2], 71), 0),
    }


floor_value = 0.05
ridge_weight = 1.0

def look_sums(first_rows, second_rows):
    first_real = first_rows[0].astype(jnp.float32)
    first_imag = first_rows[1].astype(jnp.float32)
    second_real = second_rows[0].astype(jnp.float32)
    second_imag = second_rows[1].astype(jnp.float32)
    real_part = first_real * second_real + first_imag * second_imag
    imag_part = first_imag * second_real - first_real * second_imag
    slot_count = real_part.shape[0]
    height = real_part.shape[1]
    tile_width = real_part.shape[2]
    shape_six = (slot_count, height // LOOK_AZ, LOOK_AZ, tile_width // LOOK_RG, LOOK_RG)
    real_looks = jnp.sum(real_part.reshape(shape_six), axis=(2, 4)).reshape(slot_count, -1)
    imag_looks = jnp.sum(imag_part.reshape(shape_six), axis=(2, 4)).reshape(slot_count, -1)
    return (real_looks, imag_looks)

def reweighted(phases, offsets):
    date_count = offsets.shape[0]
    is_live = offsets > 0
    second_date = jnp.arange(date_count, dtype=jnp.int32)[:, None] + offsets
    select = ((second_date[:, :, None] == jnp.arange(date_count, dtype=jnp.int32)[None, None, :]) & is_live[:, :, None]).astype(jnp.float32)
    live_weight = is_live.astype(jnp.float32)[:, :, None]
    pixels = phases.shape[2]
    series = jnp.zeros((date_count, pixels), jnp.float32)
    identity = jnp.eye(date_count, dtype=jnp.float32)
    highest = lax.Precision.HIGHEST
    for round_index in range(ITERS):
        later_values = jnp.einsum('dke,ep->dkp', select, series, precision=highest)
        residual = phases - (series[:, None, :] - later_values)
        weight = live_weight / jnp.maximum(jnp.abs(residual), floor_value)
        upper_band = jnp.einsum('dkp,dke->pde', weight, select, precision=highest)
        degree = jnp.sum(weight, axis=1).T + jnp.sum(upper_band, axis=1)
        gram_matrix = ridge_weight * identity[None] + degree[:, :, None] * identity[None] - upper_band - jnp.swapaxes(upper_band, 1, 2)
        weighted = weight * phases
        right_side = jnp.sum(weighted, axis=1) - jnp.einsum('dkp,dke->ep', weighted, select, precision=highest)
        factor = jnp.linalg.cholesky(gram_matrix)
        middle = jax.scipy.linalg.solve_triangular(factor, right_side.T[:, :, None], lower=True)
        answer = jax.scipy.linalg.solve_triangular(factor, middle, lower=True, trans=1)
        series = answer[:, :, 0].T
    return series

def tile_looks(slc, offsets, tile_index):
    tile_width = slc.shape[3] // N_TILE
    column_block = lax.dynamic_slice_in_dim(slc, tile_index * tile_width, tile_width, 3)
    date_count = offsets.shape[0]

    def per_date(date_index):
        first_rows = lax.dynamic_slice_in_dim(column_block, date_index, 1, 1)
        seconds = date_index + lax.dynamic_index_in_dim(offsets, date_index, 0, keepdims=False)
        second_rows = jnp.take(column_block, seconds.astype(jnp.int32), axis=1)
        real_looks, imag_looks = look_sums(jnp.broadcast_to(first_rows, second_rows.shape), second_rows)
        totals = jnp.stack([jnp.sum(real_looks, axis=1), jnp.sum(imag_looks, axis=1)], axis=1)
        return (jnp.arctan2(imag_looks, real_looks), totals)
    return lax.map(per_date, jnp.arange(date_count, dtype=jnp.int32))

def reference(slc, offsets):
    angles, anchors = lax.map(partial(tile_looks, slc, offsets), jnp.arange(N_TILE, dtype=jnp.int32))
    middle_tile = anchors[N_TILE // 2]
    anchor_angle = jnp.arctan2(middle_tile[..., 1], middle_tile[..., 0])
    phases = angles - anchor_angle[None, :, :, None]
    date_count = offsets.shape[0]
    look_count = phases.shape[3]
    owned_pixels = look_count // N_DATE
    blocks = phases.reshape(N_TILE, date_count, MAXP, N_DATE, owned_pixels).transpose(0, 3, 1, 2, 4)
    blocks = blocks.reshape(N_TILE * N_DATE, date_count, MAXP, owned_pixels)
    solved = lax.map(lambda block_phases: reweighted(block_phases, offsets), blocks)
    solved = solved.reshape(N_TILE, N_DATE, date_count, owned_pixels).transpose(2, 0, 1, 3)
    return solved.reshape(date_count, N_TILE, look_count)
```

```python
import jax
import jax.numpy as jnp
from jax import lax
from jax.experimental import pallas as pl
from jax.experimental.pallas import tpu as pltpu
from jax.sharding import PartitionSpec as P

LOOK_AZ = 5
LOOK_RG = 20
SPAN = 24
ITERS = 2
LANES = 128
WIN = 32

floor_value = 0.05
ridge_weight = 1.0
F32 = jnp.float32


def gather_kernel(slc_ref, out_ref, rows_ref):
    tiles = slc_ref.shape[3] // LANES
    for part in range(2):
        for date in range(8):
            base = (part * 8 + date) * 16
            block = slc_ref[part, date].astype(F32)
            for t in range(tiles):
                rows_ref[t, base:base + 10, :] = block[:, t * LANES:(t + 1) * LANES]
    lane = lax.broadcasted_iota(jnp.int32, (16, LANES), 1)

    def body(step, carry):
        half = step // 4
        quarter = step % 4
        shifted = []
        for rho in range(5):
            line = []
            for t in range(5):
                tile = quarter * 5 + t
                row = half * 5 + rho
                line.append(jnp.concatenate([
                    rows_ref[tile, pl.ds(row, 8, stride=16), :],
                    rows_ref[tile, pl.ds(128 + row, 8, stride=16), :],
                ], axis=0))
            shifted.append(line)
        moved = []
        for rho in range(5):
            amount = 20 * rho
            if amount == 0:
                moved.append(shifted[rho] + [jnp.zeros((16, LANES), F32)])
                continue
            rolled = [pltpu.roll(v, amount, 1) for v in shifted[rho]]
            line = []
            for t in range(6):
                left = rolled[t - 1] if t > 0 else jnp.zeros((16, LANES), F32)
                right = rolled[t] if t < 5 else jnp.zeros((16, LANES), F32)
                line.append(jnp.where(lane < amount, left, right))
            moved.append(line)
        for local_pixel in range(32):
            start = 20 * local_pixel
            tile, offset = start // LANES, start % LANES
            out = jnp.zeros((16, LANES), F32)
            for rho in range(5):
                lo = offset + 20 * rho
                hi = lo + 20
                if lo < LANES:
                    mask = (lane >= lo) & (lane < hi)
                    out = jnp.where(mask, moved[rho][tile], out)
                if hi > LANES:
                    mask = (lane >= lo - LANES) & (lane < hi - LANES)
                    out = jnp.where(mask, moved[rho][tile + 1], out)
            slot = half * 16 + quarter * 4 + local_pixel // 8
            out_ref[slot, local_pixel % 8] = out.astype(jnp.bfloat16)
        return carry

    lax.fori_loop(0, 8, body, 0)


def gather_samples(slc):
    cols = slc.shape[3]
    groups = 2 * cols // (8 * LOOK_RG)
    return pl.pallas_call(
        gather_kernel,
        out_shape=jax.ShapeDtypeStruct((groups, 8, 16, LANES), jnp.bfloat16),
        in_specs=[pl.BlockSpec(memory_space=pltpu.VMEM)],
        out_specs=pl.BlockSpec(memory_space=pltpu.VMEM),
        scratch_shapes=[pltpu.VMEM((cols // LANES, 256, LANES), F32)],
        name="gather_samples",
    )(slc)


def looks_kernel(samples_ref, looks_ref, anchor_ref, band_ref):
    lane = lax.broadcasted_iota(jnp.int32, (8, LANES), 1)
    contract = (((1,), (1,)), ((), ()))
    row_id = lax.broadcasted_iota(jnp.int32, (256, 256), 0)
    col_id = lax.broadcasted_iota(jnp.int32, (256, 256), 1)
    mirror = (row_id + col_id == 255).astype(F32).astype(jnp.bfloat16)
    for pixel in range(8):
        both = samples_ref[:, pixel].astype(F32)
        real = both[:, :8].reshape(256, LANES)
        imag = both[:, 8:].reshape(256, LANES)
        right = jnp.concatenate([real, imag], axis=1).astype(jnp.bfloat16)
        turned = jnp.concatenate([imag, -real], axis=1).astype(jnp.bfloat16)
        descending = jnp.dot(mirror, right, preferred_element_type=F32).astype(jnp.bfloat16)
        group, place = pixel // 4, pixel % 4
        inside = (lane >= place * WIN) & (lane < (place + 1) * WIN)
        for part, left in enumerate((right, turned)):
            gram = lax.dot_general(left, descending, contract, preferred_element_type=F32)
            for block in range(32):
                rows = gram[block * 8:block * 8 + 8, :]
                shift = (block * 8 + place * WIN + WIN) % 256
                skew = pltpu.roll(rows, shift, 1, stride=1, stride_axis=0)[:, :LANES]
                where = (part, group, pl.ds(block * 8, 8))
                if place == 0:
                    band_ref[where] = skew
                else:
                    band_ref[where] = jnp.where(inside, skew, band_ref[where])
    for part in range(2):
        for half in range(2):
            total = jnp.zeros((WIN, LANES), F32)
            for group in range(2):
                turned = band_ref[part, group, half * LANES:(half + 1) * LANES, :].T
                looks_ref[part, half, group * LANES:(group + 1) * LANES, :] = turned
                for place in range(4):
                    total = total + turned[place * WIN:(place + 1) * WIN]
            anchor_ref[part, half] = total


def pair_looks(samples):
    return pl.pallas_call(
        looks_kernel,
        out_shape=(
            jax.ShapeDtypeStruct((2, 2, 256, LANES), F32),
            jax.ShapeDtypeStruct((2, 2, WIN, LANES), F32),
        ),
        in_specs=[pl.BlockSpec(memory_space=pltpu.VMEM)],
        out_specs=(pl.BlockSpec(memory_space=pltpu.VMEM), pl.BlockSpec(memory_space=pltpu.VMEM)),
        scratch_shapes=[pltpu.VMEM((2, 2, 256, LANES), F32)],
        name="pair_looks",
    )(samples)


def factor_step(block, mat_ref, rhs_ref, low_ref, sol_ref):
    base = pl.multiple_of(block * 256, 256)

    def spread(ref, row):
        return jnp.broadcast_to(ref[pl.ds(row, 1), :], (8, LANES))

    s = {}
    for i in range(8):
        for j in range(i, 8):
            s[i, j] = spread(mat_ref, base + i * WIN + j)
    rows = []
    for i in range(8):
        tiles = [mat_ref[pl.ds(pl.multiple_of(base + i * WIN + 8 * t, 8), 8), :] for t in (1, 2, 3)]
        rows.append(tiles + [spread(rhs_ref, block * 8 + i)])
    mult = {}
    inverse = []
    for a in (0, 2, 4, 6):
        b = a + 1
        det = s[a, a] * s[b, b] - s[a, b] * s[a, b]
        scale = 1.0 / det
        e11, e12, e22 = s[b, b] * scale, -s[a, b] * scale, s[a, a] * scale
        inverse.append((e11, e12, e22))
        for i in range(a + 2, 8):
            mult[i, a] = s[a, i] * e11 + s[b, i] * e12
            mult[i, b] = s[a, i] * e12 + s[b, i] * e22
        for i in range(a + 2, 8):
            for j in range(i, 8):
                s[i, j] = s[i, j] - mult[i, a] * s[a, j] - mult[i, b] * s[b, j]
        for i in range(a + 2, 8):
            rows[i] = [rows[i][t] - mult[i, a] * rows[a][t] - mult[i, b] * rows[b][t] for t in range(4)]
    scaled = [None] * 8
    for index, a in enumerate((0, 2, 4, 6)):
        e11, e12, e22 = inverse[index]
        scaled[a] = [e11 * rows[a][t] + e12 * rows[a + 1][t] for t in range(4)]
        scaled[a + 1] = [e12 * rows[a][t] + e22 * rows[a + 1][t] for t in range(4)]
    for k in range(8):
        for t in range(3):
            low_ref[k * 24 + 8 * t:k * 24 + 8 * t + 8, :] = scaled[k][t]
    for r in range(24):
        t = r // 8
        target = pl.multiple_of((block + 1) * 256, 256) + r * WIN
        factors = [jnp.broadcast_to(low_ref[k * 24 + r:k * 24 + r + 1, :], (8, LANES)) for k in range(8)]
        for u in range(t, 3):
            where = pl.ds(pl.multiple_of(target + (u - t) * 8, 8), 8)
            value = mat_ref[where, :]
            for k in range(8):
                value = value - factors[k] * rows[k][u]
            mat_ref[where, :] = value
    for u in range(3):
        where = pl.ds(pl.multiple_of((block + 1 + u) * 8, 8), 8)
        value = rhs_ref[where, :]
        for k in range(8):
            value = value - scaled[k][3] * rows[k][u]
        rhs_ref[where, :] = value
    for a in (6, 4, 2, 0):
        for c in (a, a + 1):
            for i in range(a + 2, 8):
                scaled[c] = [scaled[c][t] - mult[i, c] * scaled[i][t] for t in range(4)]
    sub = lax.broadcasted_iota(jnp.int32, (8, LANES), 0)
    answer = scaled[0][3]
    for i in range(1, 8):
        answer = jnp.where(sub == i, scaled[i][3], answer)
    sol_ref[pl.ds(pl.multiple_of(block * 8, 8), 8), :] = answer
    for i in range(8):
        for t in range(3):
            mat_ref[pl.ds(pl.multiple_of(base + i * WIN + 8 * (t + 1), 8), 8), :] = scaled[i][t]


def back_step(block, mat_ref, sol_ref):
    base = pl.multiple_of(block * 256, 256)
    here = pl.ds(pl.multiple_of(block * 8, 8), 8)
    value = sol_ref[here, :]
    parts = []
    for c in range(23, -1, -1):
        column = mat_ref[pl.ds(base + 8 + c, 8, stride=WIN), :]
        later = jnp.broadcast_to(sol_ref[pl.ds((block + 1) * 8 + c, 1), :], (8, LANES))
        parts.append(column * later)
    while len(parts) > 1:
        parts = [parts[i] + parts[i + 1] if i + 1 < len(parts) else parts[i]
                 for i in range(0, len(parts), 2)]
    sol_ref[here, :] = value - parts[0]


def solve_kernel(looks_ref, anchor_ref, live_ref, out_ref, phase_ref, mat_ref, rhs_ref, low_ref, sol_ref):
    lane = lax.broadcasted_iota(jnp.int32, (8, LANES), 1)
    for half in range(2):
        base = jnp.arctan2(anchor_ref[1, half, :SPAN + 8, :], anchor_ref[0, half, :SPAN + 8, :])
        for pixel in range(8):
            where = slice(pixel * WIN, pixel * WIN + WIN)
            angle = jnp.arctan2(looks_ref[1, half, where, :], looks_ref[0, half, where, :])
            phase_ref[half, where, :] = angle - base
    sol_ref[...] = jnp.zeros_like(sol_ref)
    rhs_ref[...] = jnp.zeros_like(rhs_ref)
    filler = jnp.zeros((LANES - 8, LANES), F32)

    def turned(value):
        return jnp.concatenate([value, filler], axis=0).T

    def round_body(_, carry):
        now = [sol_ref[h * LANES:(h + 1) * LANES, :].T[:8] for h in range(2)]
        degree = [jnp.full((8, LANES), ridge_weight, F32) for _ in range(2)]
        right = [jnp.zeros((8, LANES), F32) for _ in range(2)]

        def clear(i, c):
            mat_ref[pl.ds(pl.multiple_of(i * WIN + 24, 8), 8), :] = jnp.zeros((8, LANES), F32)
            return c

        lax.fori_loop(0, 256, clear, 0, unroll=8)

        def ahead(pair, shift):
            a, b = (pltpu.roll(v, LANES - shift, 1) for v in pair)
            keep = lane < LANES - shift
            return [jnp.where(keep, a, b), jnp.where(keep, b, a)]

        def behind(pair, shift):
            a, b = (pltpu.roll(v, shift, 1) for v in pair)
            keep = lane >= shift
            return [jnp.where(keep, a, b), jnp.where(keep, b, a)]

        for d in range(1, SPAN + 1):
            later = ahead(now, d)
            weights, moments = [], []
            for h in range(2):
                phase = phase_ref[h, pl.ds(WIN - 1 - d, 8, stride=WIN), :]
                residual = phase - (now[h] - later[h])
                live = jnp.broadcast_to(live_ref[h, WIN - 1 - d:WIN - d, :], (8, LANES))
                weight = live / jnp.maximum(jnp.abs(residual), floor_value)
                weights.append(weight)
                moments.append(weight * phase)
            from_w, from_m = behind(weights, d), behind(moments, d)
            for h in range(2):
                degree[h] = degree[h] + (weights[h] + from_w[h])
                right[h] = right[h] + (moments[h] - from_m[h])
                column = turned(-weights[h])
                for b in range(16):
                    mat_ref[pl.ds((h * 16 + b) * 256 + d, 8, stride=WIN + 1), :] = column[b * 8:b * 8 + 8]
        for h in range(2):
            column = turned(degree[h])
            for b in range(16):
                mat_ref[pl.ds((h * 16 + b) * 256, 8, stride=WIN + 1), :] = column[b * 8:b * 8 + 8]
            rhs_ref[h * LANES:(h + 1) * LANES, :] = turned(right[h])

        def forward(i, c):
            factor_step(i, mat_ref, rhs_ref, low_ref, sol_ref)
            return c

        lax.fori_loop(0, 32, forward, 0)

        def backward(i, c):
            back_step(31 - i, mat_ref, sol_ref)
            return c

        lax.fori_loop(0, 32, backward, 0)
        return carry

    lax.fori_loop(0, ITERS, round_body, 0)
    out_ref[...] = sol_ref[:256, :8]


def solve(looks, anchor, live):
    return pl.pallas_call(
        solve_kernel,
        out_shape=jax.ShapeDtypeStruct((256, 8), F32),
        in_specs=[pl.BlockSpec(memory_space=pltpu.VMEM)] * 3,
        out_specs=pl.BlockSpec(memory_space=pltpu.VMEM),
        scratch_shapes=[
            pltpu.VMEM((2, 256, LANES), F32),
            pltpu.VMEM((280 * WIN, LANES), F32),
            pltpu.VMEM((280, LANES), F32),
            pltpu.VMEM((8 * 24, LANES), F32),
            pltpu.VMEM((280, LANES), F32),
        ],
        name="solve",
    )(looks, anchor, live)


def live_mask(offsets):
    distance = (WIN - 1 - jnp.arange(WIN, dtype=jnp.int32))[:, None, None]
    hit = jnp.any((offsets[None] == distance) & (offsets[None] > 0), axis=2)
    return hit.astype(F32).reshape(WIN, 2, LANES).transpose(1, 0, 2)


def local(slc, offsets):
    live = live_mask(offsets)
    samples = gather_samples(slc)
    samples = lax.all_to_all(samples, "date", split_axis=0, concat_axis=0, tiled=True)
    looks, partial = pair_looks(samples)
    owner = lax.axis_index("tile") == lax.axis_size("tile") // 2
    anchor = lax.psum(jnp.where(owner, partial, 0.0), ("date", "tile"))
    series = solve(looks, anchor, live)
    return series[:, None, :]


def solution(mesh):
    return jax.shard_map(
        local,
        mesh=mesh,
        in_specs=(P(None, "date", None, "tile"), P()),
        out_specs=P(None, "tile", "date"),
        check_vma=False,
    )
```

```python
import jax
import jax.numpy as jnp
from jax import lax
from jax.experimental import pallas as pl
from jax.experimental.pallas import tpu as pltpu
from jax.sharding import PartitionSpec as P

LOOK_AZ = 5
LOOK_RG = 20
SPAN = 24
ITERS = 2
LANES = 128
WIN = 32

floor_value = 0.05
ridge_weight = 1.0
F32 = jnp.float32
MESH = pl.DeviceIdType.MESH
OWNERS = 6
OWNER_STEP = 5


def gather_step(step, slc_ref, send_ref):
    lane = lax.broadcasted_iota(jnp.int32, (16, LANES), 1)
    half = step // 4
    quarter = step % 4
    blank = jnp.zeros((16, LANES), F32)
    moved = []
    for rho in range(LOOK_AZ):
        amount = LOOK_RG * rho
        line = []
        for t in range(5):
            columns = pl.ds(pl.multiple_of((quarter * 5 + t) * LANES, LANES), LANES)
            row = half * LOOK_AZ + rho
            line.append(jnp.concatenate([
                slc_ref[0, row, :, columns].astype(F32),
                slc_ref[1, row, :, columns].astype(F32),
            ], axis=0))
        if amount == 0:
            moved.append(line + [blank])
            continue
        rolled = [blank] + [pltpu.roll(v, amount, 1) for v in line] + [blank]
        moved.append([jnp.where(lane < amount, rolled[t], rolled[t + 1]) for t in range(6)])
    for local_pixel in range(32):
        start = LOOK_RG * local_pixel
        tile, offset = start // LANES, start % LANES
        out = blank
        for rho in range(LOOK_AZ):
            lo = offset + LOOK_RG * rho
            hi = lo + LOOK_RG
            if lo < LANES:
                out = jnp.where((lane >= lo) & (lane < hi), moved[rho][tile], out)
            if hi > LANES:
                mask = (lane >= lo - LANES) & (lane < hi - LANES)
                out = jnp.where(mask, moved[rho][tile + 1], out)
        slot = half * 16 + quarter * 4 + local_pixel // 8
        send_ref[slot, local_pixel % 8] = out.astype(jnp.bfloat16)


def skewed(gram_ref, index, block, place):
    rows = pl.ds(block * 8, 8)
    first = gram_ref[index + (rows, pl.ds(0, LANES))] if block >= 13 else None
    second = gram_ref[index + (rows, pl.ds(LANES, LANES))] if block < 16 else None
    if first is None:
        value = second
    elif second is None:
        value = first
    else:
        lane = lax.broadcasted_iota(jnp.int32, (8, LANES), 1)
        value = jnp.where(lane >= 64, first, second)
    shift = (place * WIN + SPAN + 1 + block * 8) % LANES
    return pltpu.roll(value, shift, 1, stride=1, stride_axis=0)


def front_kernel(slc_ref, phase_ref, send_ref, recv_ref, gram_ref, total_ref, band_ref, part_ref,
                 gathered_ref, anchor_ref, send_sem, recv_sem, part_send, part_recv, column_send,
                 column_recv, plane_send, plane_recv):
    dates = send_ref.shape[0]
    tiles = lax.axis_size("tile")
    me = lax.axis_index("date")
    tile = lax.axis_index("tile")
    middle = tiles // 2
    lane = lax.broadcasted_iota(jnp.int32, (8, LANES), 1)

    def peer(k):
        return lax.rem(me + k, dates)

    barrier = pltpu.get_barrier_semaphore()

    def greet(k, carry):
        pl.semaphore_signal(barrier, inc=1, device_id={"date": peer(k)}, device_id_type=MESH)
        return carry

    def greet_column(k, carry):
        pl.semaphore_signal(barrier, inc=1, device_id={"tile": lax.rem(tile + k, tiles)}, device_id_type=MESH)
        return carry

    lax.fori_loop(1, dates, greet, 0)
    lax.fori_loop(1, tiles, greet_column, 0)

    def gather(step, carry):
        gather_step(step, slc_ref, send_ref)
        return carry

    lax.fori_loop(0, 8, gather, 0)
    pl.semaphore_wait(barrier, dates - 1 + tiles - 1)

    def sample_copy(other, slot):
        return pltpu.make_async_remote_copy(
            src_ref=send_ref.at[other], dst_ref=recv_ref.at[slot],
            send_sem=send_sem.at[other], recv_sem=recv_sem.at[slot],
            device_id={"date": other}, device_id_type=MESH)

    def send(k, carry):
        sample_copy(peer(k), me).start()
        return carry

    lax.fori_loop(1, dates, send, 0)
    recv_ref[me] = send_ref[me]

    def arrive(k, carry):
        other = peer(k)
        sample_copy(other, other).wait_recv()
        return carry

    lax.fori_loop(1, dates, arrive, 0)

    row_id = lax.broadcasted_iota(jnp.int32, (256, 256), 0)
    col_id = lax.broadcasted_iota(jnp.int32, (256, 256), 1)
    mirror = (row_id + col_id == 255).astype(F32).astype(jnp.bfloat16)
    contract = (((1,), (1,)), ((), ()))
    total_ref[...] = jnp.zeros_like(total_ref)

    def grams(pixel, carry):
        both = recv_ref[:, pixel].astype(F32)
        real = both[:, :8].reshape(256, LANES)
        imag = both[:, 8:].reshape(256, LANES)
        right = jnp.concatenate([real, imag], axis=1).astype(jnp.bfloat16)
        turned = jnp.concatenate([imag, -real], axis=1).astype(jnp.bfloat16)
        descending = jnp.dot(mirror, right, preferred_element_type=F32).astype(jnp.bfloat16)
        for part, left in enumerate((right, turned)):
            gram = lax.dot_general(left, descending, contract, preferred_element_type=F32)
            gram_ref[pixel, part] = gram
            total_ref[part] = total_ref[part] + gram
        return carry

    lax.fori_loop(0, 8, grams, 0)

    def part_copy(owner, slot):
        return pltpu.make_async_remote_copy(
            src_ref=part_ref.at[owner], dst_ref=gathered_ref.at[slot],
            send_sem=part_send.at[owner], recv_sem=part_recv.at[slot],
            device_id={"date": owner * OWNER_STEP}, device_id_type=MESH)

    @pl.when(tile == middle)
    def _():
        for block in range(32):
            value = jnp.where(lane < WIN, skewed(total_ref, (0,), block, 0), skewed(total_ref, (1,), block, 1))
            band_ref[0, 0, block * 8:block * 8 + 8, :] = value
        for half in range(2):
            turned = band_ref[0, 0, half * LANES:(half + 1) * LANES, :].T
            for third in range(3):
                owner = half * 3 + third
                part_ref[owner, 0:8, :] = turned[third * 8:third * 8 + 8]
                part_ref[owner, 8:16, :] = turned[WIN + third * 8:WIN + third * 8 + 8]
        for owner in range(OWNERS):
            @pl.when(me != owner * OWNER_STEP)
            def _():
                part_copy(owner, me).start()

    def bands(group, carry):
        for part in range(2):
            for block in range(32):
                value = skewed(gram_ref, (group * 4, part), block, 0)
                for place in range(1, 4):
                    other = skewed(gram_ref, (group * 4 + place, part), block, place)
                    value = jnp.where(lane < place * WIN, value, other)
                band_ref[part, group, block * 8:block * 8 + 8, :] = value
        for half in range(2):
            rows = slice(half * LANES, (half + 1) * LANES)
            real = band_ref[0, group, rows, :].T
            imag = band_ref[1, group, rows, :].T
            phase_ref[half, pl.ds(pl.multiple_of(group * LANES, LANES), LANES), :] = jnp.arctan2(imag, real)
        return carry

    lax.fori_loop(0, 2, bands, 0)

    def column_copy(owner, other):
        return pltpu.make_async_remote_copy(
            src_ref=anchor_ref.at[owner], dst_ref=anchor_ref.at[owner],
            send_sem=column_send.at[other], recv_sem=column_recv.at[0],
            device_id={"tile": other}, device_id_type=MESH)

    def plane_copy(owner, other):
        return pltpu.make_async_remote_copy(
            src_ref=anchor_ref.at[owner], dst_ref=anchor_ref.at[owner],
            send_sem=plane_send.at[other], recv_sem=plane_recv.at[owner],
            device_id={"date": other}, device_id_type=MESH)

    def plane_start(owner):
        def go(k, carry):
            plane_copy(owner, peer(k)).start()
            return carry

        lax.fori_loop(1, dates, go, 0)

    for owner in range(OWNERS):
        @pl.when((me == owner * OWNER_STEP) & (tile == middle))
        def _():
            def part_arrive(k, total):
                other = peer(k)
                part_copy(owner, other).wait_recv()
                return total + gathered_ref[other]

            total = lax.fori_loop(1, dates, part_arrive, part_ref[owner])
            anchor_ref[owner] = jnp.arctan2(total[8:], total[:8])

            def go(k, carry):
                column_copy(owner, lax.rem(tile + k, tiles)).start()
                return carry

            lax.fori_loop(1, tiles, go, 0)
            plane_start(owner)

        @pl.when((me == owner * OWNER_STEP) & (tile != middle))
        def _():
            column_copy(owner, middle).wait_recv()
            plane_start(owner)

    for owner in range(OWNERS):
        @pl.when(me != owner * OWNER_STEP)
        def _():
            plane_copy(owner, owner * OWNER_STEP).wait_recv()

    for half in range(2):
        base = jnp.concatenate([anchor_ref[half * 3 + t] for t in range(3)], axis=0)
        for pixel in range(8):
            rows = slice(pixel * WIN, pixel * WIN + SPAN)
            phase_ref[half, rows, :] = phase_ref[half, rows, :] - base

    def drain(k, carry):
        sample_copy(peer(k), me).wait_send()
        return carry

    lax.fori_loop(1, dates, drain, 0)
    for owner in range(OWNERS):
        @pl.when((me != owner * OWNER_STEP) & (tile == middle))
        def _():
            part_copy(owner, me).wait_send()

        @pl.when(me == owner * OWNER_STEP)
        def _():
            def done(k, carry):
                plane_copy(owner, peer(k)).wait_send()
                return carry

            lax.fori_loop(1, dates, done, 0)

        @pl.when((me == owner * OWNER_STEP) & (tile == middle))
        def _():
            def done(k, carry):
                column_copy(owner, lax.rem(tile + k, tiles)).wait_send()
                return carry

            lax.fori_loop(1, tiles, done, 0)


def pair_phases(slc, dates, tiles):
    groups = dates
    return pl.pallas_call(
        front_kernel,
        out_shape=jax.ShapeDtypeStruct((2, 256, LANES), F32),
        in_specs=[pl.BlockSpec(memory_space=pltpu.VMEM)],
        out_specs=pl.BlockSpec(memory_space=pltpu.VMEM),
        scratch_shapes=[
            pltpu.VMEM((groups, 8, 16, LANES), jnp.bfloat16),
            pltpu.VMEM((groups, 8, 16, LANES), jnp.bfloat16),
            pltpu.VMEM((8, 2, 256, 256), F32),
            pltpu.VMEM((2, 256, 256), F32),
            pltpu.VMEM((2, 2, 256, LANES), F32),
            pltpu.VMEM((OWNERS, 16, LANES), F32),
            pltpu.VMEM((groups, 16, LANES), F32),
            pltpu.VMEM((OWNERS, 8, LANES), F32),
            pltpu.SemaphoreType.DMA((groups,)),
            pltpu.SemaphoreType.DMA((groups,)),
            pltpu.SemaphoreType.DMA((OWNERS,)),
            pltpu.SemaphoreType.DMA((groups,)),
            pltpu.SemaphoreType.DMA((tiles,)),
            pltpu.SemaphoreType.DMA((1,)),
            pltpu.SemaphoreType.DMA((groups,)),
            pltpu.SemaphoreType.DMA((OWNERS,)),
        ],
        compiler_params=pltpu.CompilerParams(collective_id=0, has_side_effects=True),
        name="pair_phases",
    )(slc)


def factor_step(block, mat_ref, rhs_ref, low_ref, sol_ref):
    base = pl.multiple_of(block * 256, 256)

    def spread(ref, row):
        return jnp.broadcast_to(ref[pl.ds(row, 1), :], (8, LANES))

    s = {}
    for i in range(8):
        for j in range(i, 8):
            s[i, j] = spread(mat_ref, base + i * WIN + j)
    rows = []
    for i in range(8):
        tiles = [mat_ref[pl.ds(pl.multiple_of(base + i * WIN + 8 * t, 8), 8), :] for t in (1, 2, 3)]
        rows.append(tiles + [spread(rhs_ref, block * 8 + i)])
    mult = {}
    inverse = []
    for a in (0, 2, 4, 6):
        b = a + 1
        det = s[a, a] * s[b, b] - s[a, b] * s[a, b]
        scale = 1.0 / det
        e11, e12, e22 = s[b, b] * scale, -s[a, b] * scale, s[a, a] * scale
        inverse.append((e11, e12, e22))
        for i in range(a + 2, 8):
            mult[i, a] = s[a, i] * e11 + s[b, i] * e12
            mult[i, b] = s[a, i] * e12 + s[b, i] * e22
        for i in range(a + 2, 8):
            for j in range(i, 8):
                s[i, j] = s[i, j] - mult[i, a] * s[a, j] - mult[i, b] * s[b, j]
        for i in range(a + 2, 8):
            rows[i] = [rows[i][t] - mult[i, a] * rows[a][t] - mult[i, b] * rows[b][t] for t in range(4)]
    scaled = [None] * 8
    for index, a in enumerate((0, 2, 4, 6)):
        e11, e12, e22 = inverse[index]
        scaled[a] = [e11 * rows[a][t] + e12 * rows[a + 1][t] for t in range(4)]
        scaled[a + 1] = [e12 * rows[a][t] + e22 * rows[a + 1][t] for t in range(4)]
    for k in range(8):
        for t in range(3):
            low_ref[k * 24 + 8 * t:k * 24 + 8 * t + 8, :] = scaled[k][t]
    for r in range(24):
        t = r // 8
        target = pl.multiple_of((block + 1) * 256, 256) + r * WIN
        factors = [jnp.broadcast_to(low_ref[k * 24 + r:k * 24 + r + 1, :], (8, LANES)) for k in range(8)]
        for u in range(t, 3):
            where = pl.ds(pl.multiple_of(target + (u - t) * 8, 8), 8)
            value = mat_ref[where, :]
            for k in range(8):
                value = value - factors[k] * rows[k][u]
            mat_ref[where, :] = value
    for u in range(3):
        where = pl.ds(pl.multiple_of((block + 1 + u) * 8, 8), 8)
        value = rhs_ref[where, :]
        for k in range(8):
            value = value - scaled[k][3] * rows[k][u]
        rhs_ref[where, :] = value
    for a in (6, 4, 2, 0):
        for c in (a, a + 1):
            for i in range(a + 2, 8):
                scaled[c] = [scaled[c][t] - mult[i, c] * scaled[i][t] for t in range(4)]
    sub = lax.broadcasted_iota(jnp.int32, (8, LANES), 0)
    answer = scaled[0][3]
    for i in range(1, 8):
        answer = jnp.where(sub == i, scaled[i][3], answer)
    sol_ref[pl.ds(pl.multiple_of(block * 8, 8), 8), :] = answer
    for i in range(8):
        for t in range(3):
            mat_ref[pl.ds(pl.multiple_of(base + i * WIN + 8 * (t + 1), 8), 8), :] = scaled[i][t]


def back_step(block, mat_ref, sol_ref):
    base = pl.multiple_of(block * 256, 256)
    here = pl.ds(pl.multiple_of(block * 8, 8), 8)
    value = sol_ref[here, :]
    parts = []
    for c in range(23, -1, -1):
        column = mat_ref[pl.ds(base + 8 + c, 8, stride=WIN), :]
        later = jnp.broadcast_to(sol_ref[pl.ds((block + 1) * 8 + c, 1), :], (8, LANES))
        parts.append(column * later)
    while len(parts) > 1:
        parts = [parts[i] + parts[i + 1] if i + 1 < len(parts) else parts[i]
                 for i in range(0, len(parts), 2)]
    sol_ref[here, :] = value - parts[0]


def solve_kernel(phase_ref, live_ref, out_ref, mat_ref, rhs_ref, low_ref, sol_ref):
    lane = lax.broadcasted_iota(jnp.int32, (8, LANES), 1)
    sol_ref[...] = jnp.zeros_like(sol_ref)
    rhs_ref[...] = jnp.zeros_like(rhs_ref)
    filler = jnp.zeros((LANES - 8, LANES), F32)

    def turned(value):
        return jnp.concatenate([value, filler], axis=0).T

    def round_body(_, carry):
        now = [sol_ref[h * LANES:(h + 1) * LANES, :].T[:8] for h in range(2)]
        degree = [jnp.full((8, LANES), ridge_weight, F32) for _ in range(2)]
        right = [jnp.zeros((8, LANES), F32) for _ in range(2)]

        def clear(i, c):
            mat_ref[pl.ds(pl.multiple_of(i * WIN + 24, 8), 8), :] = jnp.zeros((8, LANES), F32)
            return c

        lax.fori_loop(0, 256, clear, 0, unroll=8)

        def ahead(pair, shift):
            a, b = (pltpu.roll(v, LANES - shift, 1) for v in pair)
            keep = lane < LANES - shift
            return [jnp.where(keep, a, b), jnp.where(keep, b, a)]

        def behind(pair, shift):
            a, b = (pltpu.roll(v, shift, 1) for v in pair)
            keep = lane >= shift
            return [jnp.where(keep, a, b), jnp.where(keep, b, a)]

        for d in range(1, SPAN + 1):
            later = ahead(now, d)
            weights, moments = [], []
            for h in range(2):
                phase = phase_ref[h, pl.ds(SPAN - d, 8, stride=WIN), :]
                residual = phase - (now[h] - later[h])
                live = jnp.broadcast_to(live_ref[h, SPAN - d:SPAN - d + 1, :], (8, LANES))
                weight = live / jnp.maximum(jnp.abs(residual), floor_value)
                weights.append(weight)
                moments.append(weight * phase)
            from_w, from_m = behind(weights, d), behind(moments, d)
            for h in range(2):
                degree[h] = degree[h] + (weights[h] + from_w[h])
                right[h] = right[h] + (moments[h] - from_m[h])
                column = turned(-weights[h])
                for b in range(16):
                    mat_ref[pl.ds((h * 16 + b) * 256 + d, 8, stride=WIN + 1), :] = column[b * 8:b * 8 + 8]
        for h in range(2):
            column = turned(degree[h])
            for b in range(16):
                mat_ref[pl.ds((h * 16 + b) * 256, 8, stride=WIN + 1), :] = column[b * 8:b * 8 + 8]
            rhs_ref[h * LANES:(h + 1) * LANES, :] = turned(right[h])

        def forward(i, c):
            factor_step(i, mat_ref, rhs_ref, low_ref, sol_ref)
            return c

        lax.fori_loop(0, 32, forward, 0)

        def backward(i, c):
            back_step(31 - i, mat_ref, sol_ref)
            return c

        lax.fori_loop(0, 32, backward, 0)
        return carry

    lax.fori_loop(0, ITERS, round_body, 0)
    for h in range(2):
        out_ref[:, h * LANES:(h + 1) * LANES] = sol_ref[h * LANES:(h + 1) * LANES, :].T[:8]


def solve(phases, live):
    return pl.pallas_call(
        solve_kernel,
        out_shape=jax.ShapeDtypeStruct((8, 256), F32),
        in_specs=[pl.BlockSpec(memory_space=pltpu.VMEM)] * 2,
        out_specs=pl.BlockSpec(memory_space=pltpu.VMEM),
        scratch_shapes=[
            pltpu.VMEM((280 * WIN, LANES), F32),
            pltpu.VMEM((280, LANES), F32),
            pltpu.VMEM((8 * 24, LANES), F32),
            pltpu.VMEM((280, LANES), F32),
        ],
        name="solve",
    )(phases, live)


def live_mask(offsets):
    distance = (SPAN - jnp.arange(WIN, dtype=jnp.int32))[:, None, None]
    hit = jnp.any((offsets[None] == distance) & (offsets[None] > 0), axis=2)
    return hit.astype(F32).reshape(WIN, 2, LANES).transpose(1, 0, 2)


def local(slc, offsets):
    live = live_mask(offsets)
    rows_first = jnp.transpose(slc, (0, 2, 1, 3))
    phases = pair_phases(rows_first, lax.axis_size("date"), lax.axis_size("tile"))
    series = solve(phases, live)
    return series.T[:, None, :]


def solution(mesh):
    return jax.shard_map(
        local,
        mesh=mesh,
        in_specs=(P(None, "date", None, "tile"), P()),
        out_specs=P(None, "tile", "date"),
        check_vma=False,
    )
```

```python
import jax
import jax.numpy as jnp
from jax import lax
from jax.experimental import pallas as pl
from jax.experimental.pallas import tpu as pltpu
from jax.sharding import PartitionSpec as P

LOOK_AZ = 5
LOOK_RG = 20
SPAN = 24
ITERS = 2
LANES = 128
WIN = 32

floor_value = 0.05
ridge_weight = 1.0
F32 = jnp.float32
MESH = pl.DeviceIdType.MESH
OWNERS = 6
OWNER_STEP = 5


def gather_step(step, slc_ref, send_ref):
    lane = lax.broadcasted_iota(jnp.int32, (16, LANES), 1)
    half = step // 4
    quarter = step % 4
    blank = jnp.zeros((16, LANES), F32)
    moved = []
    for rho in range(LOOK_AZ):
        amount = LOOK_RG * rho
        line = []
        for t in range(5):
            columns = pl.ds(pl.multiple_of((quarter * 5 + t) * LANES, LANES), LANES)
            row = half * LOOK_AZ + rho
            line.append(jnp.concatenate([
                slc_ref[0, row, :, columns].astype(F32),
                slc_ref[1, row, :, columns].astype(F32),
            ], axis=0))
        if amount == 0:
            moved.append(line + [blank])
            continue
        rolled = [blank] + [pltpu.roll(v, amount, 1) for v in line] + [blank]
        moved.append([jnp.where(lane < amount, rolled[t], rolled[t + 1]) for t in range(6)])
    for local_pixel in range(32):
        start = LOOK_RG * local_pixel
        tile, offset = start // LANES, start % LANES
        out = blank
        for rho in range(LOOK_AZ):
            lo = offset + LOOK_RG * rho
            hi = lo + LOOK_RG
            if lo < LANES:
                out = jnp.where((lane >= lo) & (lane < hi), moved[rho][tile], out)
            if hi > LANES:
                mask = (lane >= lo - LANES) & (lane < hi - LANES)
                out = jnp.where(mask, moved[rho][tile + 1], out)
        slot = half * 16 + quarter * 4 + local_pixel // 8
        send_ref[slot, local_pixel % 8] = out.astype(jnp.bfloat16)


def skewed(gram_ref, index, block, place):
    rows = pl.ds(block * 8, 8)
    first = gram_ref[index + (rows, pl.ds(0, LANES))] if block >= 13 else None
    second = gram_ref[index + (rows, pl.ds(LANES, LANES))] if block < 16 else None
    if first is None:
        value = second
    elif second is None:
        value = first
    else:
        lane = lax.broadcasted_iota(jnp.int32, (8, LANES), 1)
        value = jnp.where(lane >= 64, first, second)
    shift = (place * WIN + SPAN + 1 + block * 8) % LANES
    return pltpu.roll(value, shift, 1, stride=1, stride_axis=0)


def front_kernel(slc_ref, phase_ref, send_ref, recv_ref, gram_ref, total_ref, band_ref, part_ref,
                 gathered_ref, anchor_ref, send_sem, recv_sem, part_send, part_recv, column_send,
                 column_recv, plane_send, plane_recv):
    dates = send_ref.shape[0]
    tiles = lax.axis_size("tile")
    me = lax.axis_index("date")
    tile = lax.axis_index("tile")
    middle = tiles // 2
    lane = lax.broadcasted_iota(jnp.int32, (8, LANES), 1)

    def peer(k):
        return lax.rem(me + k, dates)

    barrier = pltpu.get_barrier_semaphore()

    def greet(k, carry):
        pl.semaphore_signal(barrier, inc=1, device_id={"date": peer(k)}, device_id_type=MESH)
        return carry

    def greet_column(k, carry):
        pl.semaphore_signal(barrier, inc=1, device_id={"tile": lax.rem(tile + k, tiles)}, device_id_type=MESH)
        return carry

    lax.fori_loop(1, dates, greet, 0)
    lax.fori_loop(1, tiles, greet_column, 0)

    def gather(step, carry):
        gather_step(step, slc_ref, send_ref)
        return carry

    lax.fori_loop(0, 8, gather, 0)
    pl.semaphore_wait(barrier, dates - 1 + tiles - 1)

    def sample_copy(other, slot):
        return pltpu.make_async_remote_copy(
            src_ref=send_ref.at[other], dst_ref=recv_ref.at[slot],
            send_sem=send_sem.at[other], recv_sem=recv_sem.at[slot],
            device_id={"date": other}, device_id_type=MESH)

    def send(k, carry):
        sample_copy(peer(k), me).start()
        return carry

    lax.fori_loop(1, dates, send, 0)
    recv_ref[me] = send_ref[me]

    def arrive(k, carry):
        other = peer(k)
        sample_copy(other, other).wait_recv()
        return carry

    lax.fori_loop(1, dates, arrive, 0)

    row_id = lax.broadcasted_iota(jnp.int32, (256, 256), 0)
    col_id = lax.broadcasted_iota(jnp.int32, (256, 256), 1)
    mirror = (row_id + col_id == 255).astype(F32).astype(jnp.bfloat16)
    contract = (((1,), (1,)), ((), ()))
    total_ref[...] = jnp.zeros_like(total_ref)

    def grams(pixel, carry):
        both = recv_ref[:, pixel].astype(F32)
        real = both[:, :8].reshape(256, LANES)
        imag = both[:, 8:].reshape(256, LANES)
        right = jnp.concatenate([real, imag], axis=1).astype(jnp.bfloat16)
        turned = jnp.concatenate([imag, -real], axis=1).astype(jnp.bfloat16)
        descending = jnp.dot(mirror, right, preferred_element_type=F32).astype(jnp.bfloat16)
        for part, left in enumerate((right, turned)):
            gram = lax.dot_general(left, descending, contract, preferred_element_type=F32)
            gram_ref[pixel, part] = gram
            total_ref[part] = total_ref[part] + gram
        return carry

    lax.fori_loop(0, 8, grams, 0)

    def part_copy(owner, slot):
        return pltpu.make_async_remote_copy(
            src_ref=part_ref.at[owner], dst_ref=gathered_ref.at[slot],
            send_sem=part_send.at[owner], recv_sem=part_recv.at[slot],
            device_id={"date": owner * OWNER_STEP}, device_id_type=MESH)

    @pl.when(tile == middle)
    def _():
        for block in range(32):
            value = jnp.where(lane < WIN, skewed(total_ref, (0,), block, 0), skewed(total_ref, (1,), block, 1))
            band_ref[0, 0, block * 8:block * 8 + 8, :] = value
        for half in range(2):
            turned = band_ref[0, 0, half * LANES:(half + 1) * LANES, :].T
            for third in range(3):
                owner = half * 3 + third
                part_ref[owner, 0:8, :] = turned[third * 8:third * 8 + 8]
                part_ref[owner, 8:16, :] = turned[WIN + third * 8:WIN + third * 8 + 8]
        for owner in range(OWNERS):
            @pl.when(me != owner * OWNER_STEP)
            def _():
                part_copy(owner, me).start()

    def bands(group, carry):
        for part in range(2):
            for block in range(32):
                value = skewed(gram_ref, (group * 4, part), block, 0)
                for place in range(1, 4):
                    other = skewed(gram_ref, (group * 4 + place, part), block, place)
                    value = jnp.where(lane < place * WIN, value, other)
                band_ref[part, group, block * 8:block * 8 + 8, :] = value
        for half in range(2):
            rows = slice(half * LANES, (half + 1) * LANES)
            real = band_ref[0, group, rows, :].T
            imag = band_ref[1, group, rows, :].T
            phase_ref[half, pl.ds(pl.multiple_of(group * LANES, LANES), LANES), :] = jnp.arctan2(imag, real)
        return carry

    lax.fori_loop(0, 2, bands, 0)

    def column_copy(owner, other):
        return pltpu.make_async_remote_copy(
            src_ref=anchor_ref.at[owner], dst_ref=anchor_ref.at[owner],
            send_sem=column_send.at[other], recv_sem=column_recv.at[0],
            device_id={"tile": other}, device_id_type=MESH)

    def plane_copy(owner, other):
        return pltpu.make_async_remote_copy(
            src_ref=anchor_ref.at[owner], dst_ref=anchor_ref.at[owner],
            send_sem=plane_send.at[other], recv_sem=plane_recv.at[owner],
            device_id={"date": other}, device_id_type=MESH)

    def plane_start(owner):
        def go(k, carry):
            plane_copy(owner, peer(k)).start()
            return carry

        lax.fori_loop(1, dates, go, 0)

    for owner in range(OWNERS):
        @pl.when((me == owner * OWNER_STEP) & (tile == middle))
        def _():
            def part_arrive(k, total):
                other = peer(k)
                part_copy(owner, other).wait_recv()
                return total + gathered_ref[other]

            total = lax.fori_loop(1, dates, part_arrive, part_ref[owner])
            anchor_ref[owner] = jnp.arctan2(total[8:], total[:8])

            def go(k, carry):
                column_copy(owner, lax.rem(tile + k, tiles)).start()
                return carry

            lax.fori_loop(1, tiles, go, 0)
            plane_start(owner)

        @pl.when((me == owner * OWNER_STEP) & (tile != middle))
        def _():
            column_copy(owner, middle).wait_recv()
            plane_start(owner)

    for owner in range(OWNERS):
        @pl.when(me != owner * OWNER_STEP)
        def _():
            plane_copy(owner, owner * OWNER_STEP).wait_recv()

    for half in range(2):
        base = jnp.concatenate([anchor_ref[half * 3 + t] for t in range(3)], axis=0)
        for pixel in range(8):
            rows = slice(pixel * WIN, pixel * WIN + SPAN)
            phase_ref[half, rows, :] = phase_ref[half, rows, :] - base

    def drain(k, carry):
        sample_copy(peer(k), me).wait_send()
        return carry

    lax.fori_loop(1, dates, drain, 0)
    for owner in range(OWNERS):
        @pl.when((me != owner * OWNER_STEP) & (tile == middle))
        def _():
            part_copy(owner, me).wait_send()

        @pl.when(me == owner * OWNER_STEP)
        def _():
            def done(k, carry):
                plane_copy(owner, peer(k)).wait_send()
                return carry

            lax.fori_loop(1, dates, done, 0)

        @pl.when((me == owner * OWNER_STEP) & (tile == middle))
        def _():
            def done(k, carry):
                column_copy(owner, lax.rem(tile + k, tiles)).wait_send()
                return carry

            lax.fori_loop(1, tiles, done, 0)


def pair_phases(slc, dates, tiles):
    groups = dates
    return pl.pallas_call(
        front_kernel,
        out_shape=jax.ShapeDtypeStruct((2, 256, LANES), F32),
        in_specs=[pl.BlockSpec(memory_space=pltpu.VMEM)],
        out_specs=pl.BlockSpec(memory_space=pltpu.VMEM),
        scratch_shapes=[
            pltpu.VMEM((groups, 8, 16, LANES), jnp.bfloat16),
            pltpu.VMEM((groups, 8, 16, LANES), jnp.bfloat16),
            pltpu.VMEM((8, 2, 256, 256), F32),
            pltpu.VMEM((2, 256, 256), F32),
            pltpu.VMEM((2, 2, 256, LANES), F32),
            pltpu.VMEM((OWNERS, 16, LANES), F32),
            pltpu.VMEM((groups, 16, LANES), F32),
            pltpu.VMEM((OWNERS, 8, LANES), F32),
            pltpu.SemaphoreType.DMA((groups,)),
            pltpu.SemaphoreType.DMA((groups,)),
            pltpu.SemaphoreType.DMA((OWNERS,)),
            pltpu.SemaphoreType.DMA((groups,)),
            pltpu.SemaphoreType.DMA((tiles,)),
            pltpu.SemaphoreType.DMA((1,)),
            pltpu.SemaphoreType.DMA((groups,)),
            pltpu.SemaphoreType.DMA((OWNERS,)),
        ],
        compiler_params=pltpu.CompilerParams(collective_id=0, has_side_effects=True),
        name="pair_phases",
    )(slc)


def factor_step(block, mat_ref, rhs_ref, low_ref, back_ref, sol_ref):
    base = pl.multiple_of(block * 256, 256)

    def spread(ref, row):
        return jnp.broadcast_to(ref[pl.ds(row, 1), :], (8, LANES))

    s = {}
    for i in range(8):
        for j in range(i, 8):
            s[i, j] = spread(mat_ref, base + i * WIN + j)
    rows = []
    for i in range(8):
        tiles = [mat_ref[pl.ds(pl.multiple_of(base + i * WIN + 8 * t, 8), 8), :] for t in (1, 2, 3)]
        rows.append(tiles + [spread(rhs_ref, block * 8 + i)])
    mult = {}
    inverse = []
    for a in (0, 2, 4, 6):
        b = a + 1
        det = s[a, a] * s[b, b] - s[a, b] * s[a, b]
        scale = 1.0 / det
        e11, e12, e22 = s[b, b] * scale, -s[a, b] * scale, s[a, a] * scale
        inverse.append((e11, e12, e22))
        for i in range(a + 2, 8):
            mult[i, a] = s[a, i] * e11 + s[b, i] * e12
            mult[i, b] = s[a, i] * e12 + s[b, i] * e22
        for i in range(a + 2, 8):
            for j in range(i, 8):
                s[i, j] = s[i, j] - mult[i, a] * s[a, j] - mult[i, b] * s[b, j]
        for i in range(a + 2, 8):
            rows[i] = [rows[i][t] - mult[i, a] * rows[a][t] - mult[i, b] * rows[b][t] for t in range(4)]
    scaled = [None] * 8
    for index, a in enumerate((0, 2, 4, 6)):
        e11, e12, e22 = inverse[index]
        scaled[a] = [e11 * rows[a][t] + e12 * rows[a + 1][t] for t in range(4)]
        scaled[a + 1] = [e12 * rows[a][t] + e22 * rows[a + 1][t] for t in range(4)]
    for k in range(8):
        for t in range(3):
            low_ref[k * 24 + 8 * t:k * 24 + 8 * t + 8, :] = scaled[k][t]
    for r in range(24):
        t = r // 8
        target = pl.multiple_of((block + 1) * 256, 256) + r * WIN
        factors = [jnp.broadcast_to(low_ref[k * 24 + r:k * 24 + r + 1, :], (8, LANES)) for k in range(8)]
        for u in range(t, 3):
            where = pl.ds(pl.multiple_of(target + (u - t) * 8, 8), 8)
            value = mat_ref[where, :]
            for k in range(8):
                value = value - factors[k] * rows[k][u]
            mat_ref[where, :] = value
    for u in range(3):
        where = pl.ds(pl.multiple_of((block + 1 + u) * 8, 8), 8)
        value = rhs_ref[where, :]
        for k in range(8):
            value = value - scaled[k][3] * rows[k][u]
        rhs_ref[where, :] = value
    for a in (6, 4, 2, 0):
        for c in (a, a + 1):
            for i in range(a + 2, 8):
                scaled[c] = [scaled[c][t] - mult[i, c] * scaled[i][t] for t in range(4)]
    sub = lax.broadcasted_iota(jnp.int32, (8, LANES), 0)
    answer = scaled[0][3]
    for i in range(1, 8):
        answer = jnp.where(sub == i, scaled[i][3], answer)
    sol_ref[pl.ds(pl.multiple_of(block * 8, 8), 8), :] = answer
    for i in range(8):
        for t in range(3):
            back_ref[pl.ds((block * 24 + 8 * t) * 9 + i, 8, stride=9), :] = scaled[i][t]


def tree_sum(parts):
    while len(parts) > 1:
        parts = [parts[i] + parts[i + 1] if i + 1 < len(parts) else parts[i]
                 for i in range(0, len(parts), 2)]
    return parts[0]


def back_step(block, back_ref, sol_ref):
    rows = slice(block * 8, block * 8 + 8)

    def product(c):
        start = (block * 24 + c) * 9
        later = jnp.broadcast_to(sol_ref[block * 8 + 8 + c:block * 8 + 9 + c, :], (8, LANES))
        return back_ref[pl.ds(start, 8), :] * later

    value = sol_ref[rows, :] - tree_sum([product(c) for c in range(8, 24)])
    sol_ref[rows, :] = value - tree_sum([product(c) for c in range(8)])


ENDS = 14
LAST = 17


def join_ends(mat_ref, rhs_ref, tmp_ref):
    mine = lax.broadcasted_iota(jnp.int32, (8, LANES), 1) < 8
    for first in range(ENDS, LAST):
        for second in range(first, LAST):
            u = second - first
            for row in range(8):
                start = (first * 8 + row) * WIN + 8 * u
                value = jnp.where(mine, pltpu.roll(mat_ref[start:start + 8, :], LANES - 8, 1), 0.0)
                tmp_ref[pl.ds(7 - row, 8, stride=9), :] = value
            for row in range(8):
                start = ((31 - second) * 8 + row) * WIN + 8 * u
                mat_ref[start:start + 8, :] = mat_ref[start:start + 8, :] + tmp_ref[pl.ds((7 - row) * 9, 8), :]
        value = jnp.where(mine, pltpu.roll(rhs_ref[first * 8:first * 8 + 8, :], LANES - 8, 1), 0.0)
        for row in range(8):
            tmp_ref[80 + 7 - row:80 + 8 - row, :] = value[row:row + 1]
        start = (31 - first) * 8
        rhs_ref[start:start + 8, :] = rhs_ref[start:start + 8, :] + tmp_ref[80:88, :]


def spread_middle(sol_ref, tmp_ref):
    lane = lax.broadcasted_iota(jnp.int32, (8, LANES), 1)
    for block in range(ENDS, LAST + 1):
        value = pltpu.roll(sol_ref[block * 8:block * 8 + 8, :], 8, 1)
        for row in range(8):
            where = (LAST - block) * 8 + 7 - row
            tmp_ref[where:where + 1, :] = value[row:row + 1]
    for block in range(ENDS, LAST + 1):
        other = tmp_ref[(block - ENDS) * 8:(block - ENDS) * 8 + 8, :]
        rows = slice(block * 8, block * 8 + 8)
        sol_ref[rows, :] = jnp.where(lane < 8, sol_ref[rows, :], other)


def solve_kernel(phase_ref, offset_ref, out_ref, live_ref, mat_ref, rhs_ref, low_ref, back_ref, sol_ref, tmp_ref):
    lane = lax.broadcasted_iota(jnp.int32, (8, LANES), 1)
    backwards = LANES - 1 - lane

    def flipped(value):
        return jnp.take_along_axis(value, backwards, axis=1, mode="promise_in_bounds")

    distance = SPAN - lax.broadcasted_iota(jnp.int32, (SPAN, LANES), 0)
    for h in range(2):
        hit = jnp.zeros((SPAN, LANES), F32)
        for k in range(offset_ref.shape[0]):
            entry = jnp.broadcast_to(offset_ref[k:k + 1, h * LANES:(h + 1) * LANES], (SPAN, LANES))
            hit = jnp.where(entry == distance, 1.0, hit)
        live_ref[h] = hit
    sol_ref[...] = jnp.zeros_like(sol_ref)
    blank = jnp.zeros((8, LANES), F32)

    def turned(pairs):
        rows = []
        for low, high in pairs:
            rows += [low, flipped(high)]
        rows += [blank] * (16 - len(rows))
        return jnp.concatenate(rows, axis=0).T

    def current():
        value = sol_ref[0:LANES, :].T
        return [value[:8], flipped(value[8:16])]

    def ahead(pair, shift):
        a, b = (pltpu.roll(v, LANES - shift, 1) for v in pair)
        keep = lane < LANES - shift
        return [jnp.where(keep, a, b), jnp.where(keep, b, a)]

    def behind(pair, shift):
        a, b = (pltpu.roll(v, shift, 1) for v in pair)
        keep = lane >= shift
        return [jnp.where(keep, a, b), jnp.where(keep, b, a)]

    def round_body(_, carry):
        now = current()
        degree = [jnp.full((8, LANES), ridge_weight, F32) for _ in range(2)]
        right = [jnp.zeros((8, LANES), F32) for _ in range(2)]
        zero = jnp.zeros((8, LANES), F32)
        for row in range(LANES):
            mat_ref[row * WIN + 24:row * WIN + 32, :] = zero
        for row in range(LANES, 144):
            for t in range(4):
                mat_ref[row * WIN + 8 * t:row * WIN + 8 * t + 8, :] = zero
        rhs_ref[128:136, :] = zero
        rhs_ref[136:144, :] = zero

        stack = []
        for d in range(1, SPAN + 1):
            later = ahead(now, d)
            weights, moments = [], []
            for h in range(2):
                phase = phase_ref[h, pl.ds(SPAN - d, 8, stride=WIN), :]
                residual = phase - (now[h] - later[h])
                live = jnp.broadcast_to(live_ref[h, SPAN - d:SPAN - d + 1, :], (8, LANES))
                weight = live / jnp.maximum(jnp.abs(residual), floor_value)
                weights.append(weight)
                moments.append(weight * phase)
            from_w, from_m = behind(weights, d), behind(moments, d)
            for h in range(2):
                degree[h] = degree[h] + (weights[h] + from_w[h])
                right[h] = right[h] + (moments[h] - from_m[h])
            crossing = jnp.where(lane < min(d, 16), 0.0, from_w[1])
            stack.append((-weights[0], -crossing))
            if len(stack) == 8:
                columns = turned(stack)
                for e in range(8):
                    column = columns if e == 0 else pltpu.roll(columns, LANES - 16 * e, 1)
                    for b in range(16):
                        where = pl.ds(b * 256 + d - 7 + e, 8, stride=WIN + 1)
                        mat_ref[where, :] = column[b * 8:b * 8 + 8]
                stack = []
        columns = turned([degree, right])
        for b in range(16):
            mat_ref[pl.ds(b * 256, 8, stride=WIN + 1), :] = columns[b * 8:b * 8 + 8]
        rhs_ref[0:LANES, :] = pltpu.roll(columns, LANES - 16, 1)

        def forward(i, c):
            factor_step(i, mat_ref, rhs_ref, low_ref, back_ref, sol_ref)
            return c

        lax.fori_loop(0, ENDS, forward, 0)
        join_ends(mat_ref, rhs_ref, tmp_ref)
        lax.fori_loop(ENDS, LAST + 1, forward, 0)

        for block in range(LAST, ENDS - 1, -1):
            back_step(block, back_ref, sol_ref)
        spread_middle(sol_ref, tmp_ref)
        for block in range(ENDS - 1, -1, -1):
            back_step(block, back_ref, sol_ref)
        return carry

    lax.fori_loop(0, ITERS, round_body, 0)
    now = current()
    for h in range(2):
        out_ref[:, h * LANES:(h + 1) * LANES] = now[h]


def solve(phases, offsets):
    return pl.pallas_call(
        solve_kernel,
        out_shape=jax.ShapeDtypeStruct((8, 256), F32),
        in_specs=[pl.BlockSpec(memory_space=pltpu.VMEM)] * 2,
        out_specs=pl.BlockSpec(memory_space=pltpu.VMEM),
        scratch_shapes=[
            pltpu.VMEM((2, SPAN, LANES), F32),
            pltpu.VMEM((168 * WIN, LANES), F32),
            pltpu.VMEM((168, LANES), F32),
            pltpu.VMEM((8 * 24, LANES), F32),
            pltpu.VMEM((18 * 24 * 9, LANES), F32),
            pltpu.VMEM((168, LANES), F32),
            pltpu.VMEM((96, LANES), F32),
        ],
        name="solve",
    )(phases, offsets)


def local(slc, offsets):
    rows_first = jnp.transpose(slc, (0, 2, 1, 3))
    phases = pair_phases(rows_first, lax.axis_size("date"), lax.axis_size("tile"))
    series = solve(phases, offsets.T)
    return series.T[:, None, :]


def solution(mesh):
    return jax.shard_map(
        local,
        mesh=mesh,
        in_specs=(P(None, "date", None, "tile"), P()),
        out_specs=P(None, "tile", "date"),
        check_vma=False,
    )
```

```python
import jax
import jax.numpy as jnp
from jax import lax
from jax.experimental import pallas as pl
from jax.experimental.pallas import tpu as pltpu
from jax.sharding import PartitionSpec as P

LOOK_AZ = 5
LOOK_RG = 20
SPAN = 24
ITERS = 2
LANES = 128
WIN = 32

floor_value = 0.05
ridge_weight = 1.0
F32 = jnp.float32
MESH = pl.DeviceIdType.MESH
OWNERS = 12
OWNER_STEP = 5
OWNER_INVERSE = 13
GROUPS = 1
RING = 4


def gather_step(step, slc_ref, send_ref):
    lane = lax.broadcasted_iota(jnp.int32, (16, LANES), 1)
    half = step // 4
    quarter = step % 4
    blank = jnp.zeros((16, LANES), F32)
    moved = []
    for rho in range(LOOK_AZ):
        amount = LOOK_RG * rho
        line = []
        for t in range(5):
            columns = pl.ds(pl.multiple_of((quarter * 5 + t) * LANES, LANES), LANES)
            row = half * LOOK_AZ + rho
            line.append(jnp.concatenate([
                slc_ref[0, row, :, columns].astype(F32),
                slc_ref[1, row, :, columns].astype(F32),
            ], axis=0))
        if amount == 0:
            moved.append(line + [blank])
            continue
        rolled = [blank] + [pltpu.roll(v, amount, 1) for v in line] + [blank]
        moved.append([jnp.where(lane < amount, rolled[t], rolled[t + 1]) for t in range(6)])
    for local_pixel in range(32):
        start = LOOK_RG * local_pixel
        tile, offset = start // LANES, start % LANES
        out = blank
        for rho in range(LOOK_AZ):
            lo = offset + LOOK_RG * rho
            hi = lo + LOOK_RG
            if lo < LANES:
                out = jnp.where((lane >= lo) & (lane < hi), moved[rho][tile], out)
            if hi > LANES:
                mask = (lane >= lo - LANES) & (lane < hi - LANES)
                out = jnp.where(mask, moved[rho][tile + 1], out)
        slot = half * 16 + quarter * 4 + local_pixel // 8
        send_ref[slot, local_pixel % 8] = out.astype(jnp.bfloat16)


def skewed(gram_ref, index, block, place):
    rows = pl.ds(block * 8, 8)
    first = gram_ref[index + (rows, pl.ds(0, LANES))] if block >= 13 else None
    second = gram_ref[index + (rows, pl.ds(LANES, LANES))] if block < 16 else None
    if first is None:
        value = second
    elif second is None:
        value = first
    else:
        lane = lax.broadcasted_iota(jnp.int32, (8, LANES), 1)
        value = jnp.where(lane >= 64, first, second)
    shift = (place * WIN + SPAN + 1 + block * 8) % LANES
    return pltpu.roll(value, shift, 1, stride=1, stride_axis=0)


def front_kernel(slc_hbm, phase_ref, slc_ref, send_ref, recv_ref, gram_ref, total_ref, band_ref,
                 part_ref, gathered_ref, anchor_ref, load_sem, send_sem, recv_sem, part_send,
                 part_recv, column_send, column_recv, plane_send, plane_recv):
    dates = send_ref.shape[0]
    tiles = lax.axis_size("tile")
    me = lax.axis_index("date")
    tile = lax.axis_index("tile")
    middle = tiles // 2
    pixels = 8 // GROUPS
    lane = lax.broadcasted_iota(jnp.int32, (8, LANES), 1)
    load = pltpu.make_async_copy(slc_hbm, slc_ref, load_sem)
    load.start()

    def peer(k):
        return me ^ (dates - 1 - k)

    def for_peers(action):
        def go(k, carry):
            action(peer(k))
            return carry

        lax.fori_loop(0, dates - 1, go, 0, unroll=True)

    def for_far_peers(action):
        steps = [(dx, dy, dc) for dx in range(RING) for dy in range(RING) for dc in range(2)]
        steps.sort(key=lambda v: -(min(v[0], RING - v[0]) + min(v[1], RING - v[1]) + v[2] / 4))
        for dx, dy, dc in steps[:-1]:
            across = (me // (2 * RING) + dx) % RING
            along = (me // 2 + dy) % RING
            core = (me + dc) % 2
            action((across * RING + along) * 2 + core)

    def for_column(action):
        def go(k, carry):
            action(lax.rem(tile + k, tiles))
            return carry

        lax.fori_loop(1, tiles, go, 0)

    barrier = pltpu.get_barrier_semaphore()
    for_column(lambda other: pl.semaphore_signal(
        barrier, inc=1, device_id={"tile": other}, device_id_type=MESH))
    for_peers(lambda other: pl.semaphore_signal(
        barrier, inc=1, device_id={"date": other}, device_id_type=MESH))
    load.wait()

    def gather(step, carry):
        gather_step(step, slc_ref, send_ref)
        return carry

    lax.fori_loop(0, 8, gather, 0)
    pl.semaphore_wait(barrier, dates - 1 + tiles - 1)

    def sample_copy(group, other, slot):
        part = pl.ds(group * pixels, pixels)
        return pltpu.make_async_remote_copy(
            src_ref=send_ref.at[other, part], dst_ref=recv_ref.at[slot, part],
            send_sem=send_sem.at[group, other], recv_sem=recv_sem.at[group, slot],
            device_id={"date": other}, device_id_type=MESH)

    for group in range(GROUPS):
        for_far_peers(lambda other: sample_copy(group, other, me).start())
    recv_ref[me] = send_ref[me]

    row_id = lax.broadcasted_iota(jnp.int32, (256, 256), 0)
    col_id = lax.broadcasted_iota(jnp.int32, (256, 256), 1)
    mirror = (row_id + col_id == 255).astype(F32).astype(jnp.bfloat16)
    contract = (((1,), (1,)), ((), ()))

    for group in range(GROUPS):
        for_peers(lambda other: sample_copy(group, other, other).wait_recv())
        total = [None, None]
        for pixel in range(group * pixels, (group + 1) * pixels):
            both = recv_ref[:, pixel].astype(F32)
            real = both[:, :8].reshape(256, LANES)
            imag = both[:, 8:].reshape(256, LANES)
            right = jnp.concatenate([real, imag], axis=1).astype(jnp.bfloat16)
            turned = jnp.concatenate([imag, -real], axis=1).astype(jnp.bfloat16)
            descending = jnp.dot(mirror, right, preferred_element_type=F32).astype(jnp.bfloat16)
            for part, left in enumerate((right, turned)):
                gram = lax.dot_general(left, descending, contract, preferred_element_type=F32)
                gram_ref[pixel, part] = gram
                if pixel == 0:
                    total_ref[part] = gram
                else:
                    total_ref[part] = total_ref[part] + gram

    def owner_date(owner):
        return lax.rem(owner * OWNER_STEP, dates)

    owned = lax.rem(me * OWNER_INVERSE, dates)

    def part_copy(owner, slot):
        return pltpu.make_async_remote_copy(
            src_ref=part_ref.at[owner], dst_ref=gathered_ref.at[slot],
            send_sem=part_send.at[owner], recv_sem=part_recv.at[slot],
            device_id={"date": owner_date(owner)}, device_id_type=MESH)

    def for_owners(action):
        def go(owner, carry):
            @pl.when(owner != owned)
            def _():
                action(owner)

            return carry

        lax.fori_loop(0, OWNERS, go, 0, unroll=True)

    @pl.when(tile == middle)
    def _():
        for block in range(32):
            value = jnp.where(lane < WIN, skewed(total_ref, (0,), block, 0), skewed(total_ref, (1,), block, 1))
            band_ref[0, 0, block * 8:block * 8 + 8, :] = value
        for half in range(2):
            turned = band_ref[0, 0, half * LANES:(half + 1) * LANES, :].T
            for sixth in range(6):
                owner = half * 6 + sixth
                part_ref[owner, 0:4, :] = turned[sixth * 4:sixth * 4 + 4]
                part_ref[owner, 4:8, :] = turned[WIN + sixth * 4:WIN + sixth * 4 + 4]
        for_owners(lambda owner: part_copy(owner, me).start())

    def bands(group, carry):
        for part in range(2):
            for block in range(32):
                value = skewed(gram_ref, (group * 4, part), block, 0)
                for place in range(1, 4):
                    other = skewed(gram_ref, (group * 4 + place, part), block, place)
                    value = jnp.where(lane < place * WIN, value, other)
                band_ref[part, group, block * 8:block * 8 + 8, :] = value
        for half in range(2):
            rows = slice(half * LANES, (half + 1) * LANES)
            real = band_ref[0, group, rows, :].T
            imag = band_ref[1, group, rows, :].T
            phase_ref[half, pl.ds(pl.multiple_of(group * LANES, LANES), LANES), :] = jnp.arctan2(imag, real)
        return carry

    lax.fori_loop(0, 2, bands, 0)

    def column_copy(owner, other):
        return pltpu.make_async_remote_copy(
            src_ref=anchor_ref.at[owner], dst_ref=anchor_ref.at[owner],
            send_sem=column_send.at[other], recv_sem=column_recv.at[0],
            device_id={"tile": other}, device_id_type=MESH)

    def plane_copy(owner, other):
        return pltpu.make_async_remote_copy(
            src_ref=anchor_ref.at[owner], dst_ref=anchor_ref.at[owner],
            send_sem=plane_send.at[other], recv_sem=plane_recv.at[owner],
            device_id={"date": other}, device_id_type=MESH)

    @pl.when((owned < OWNERS) & (tile == middle))
    def _():
        def part_arrive(k, total):
            other = peer(k)
            part_copy(owned, other).wait_recv()
            return total + gathered_ref[other]

        total = lax.fori_loop(0, dates - 1, part_arrive, part_ref[owned])
        anchor_ref[owned] = jnp.arctan2(total[4:], total[:4])
        for_column(lambda other: column_copy(owned, other).start())

    @pl.when((owned < OWNERS) & (tile != middle))
    def _():
        column_copy(owned, middle).wait_recv()

    @pl.when(owned < OWNERS)
    def _():
        for_far_peers(lambda other: plane_copy(owned, other).start())

    for group in range(GROUPS):
        for_peers(lambda other: sample_copy(group, other, me).wait_send())

    @pl.when(tile == middle)
    def _():
        for_owners(lambda owner: part_copy(owner, me).wait_send())

    for_owners(lambda owner: plane_copy(owner, owner_date(owner)).wait_recv())

    for half in range(2):
        base = jnp.concatenate([anchor_ref[half * 6 + t] for t in range(6)], axis=0)
        for pixel in range(8):
            rows = slice(pixel * WIN, pixel * WIN + SPAN)
            phase_ref[half, rows, :] = phase_ref[half, rows, :] - base

    @pl.when(owned < OWNERS)
    def _():
        for_peers(lambda other: plane_copy(owned, other).wait_send())

    @pl.when((owned < OWNERS) & (tile == middle))
    def _():
        for_column(lambda other: column_copy(owned, other).wait_send())


def pair_phases(slc, dates, tiles):
    return pl.pallas_call(
        front_kernel,
        out_shape=jax.ShapeDtypeStruct((2, 256, LANES), F32),
        in_specs=[pl.BlockSpec(memory_space=pl.ANY)],
        out_specs=pl.BlockSpec(memory_space=pltpu.VMEM),
        scratch_shapes=[
            pltpu.VMEM(slc.shape, slc.dtype),
            pltpu.VMEM((dates, 8, 16, LANES), jnp.bfloat16),
            pltpu.VMEM((dates, 8, 16, LANES), jnp.bfloat16),
            pltpu.VMEM((8, 2, 256, 256), F32),
            pltpu.VMEM((2, 256, 256), F32),
            pltpu.VMEM((2, 2, 256, LANES), F32),
            pltpu.VMEM((OWNERS, 8, LANES), F32),
            pltpu.VMEM((dates, 8, LANES), F32),
            pltpu.VMEM((OWNERS, 4, LANES), F32),
            pltpu.SemaphoreType.DMA(()),
            pltpu.SemaphoreType.DMA((GROUPS, dates)),
            pltpu.SemaphoreType.DMA((GROUPS, dates)),
            pltpu.SemaphoreType.DMA((OWNERS,)),
            pltpu.SemaphoreType.DMA((dates,)),
            pltpu.SemaphoreType.DMA((tiles,)),
            pltpu.SemaphoreType.DMA((1,)),
            pltpu.SemaphoreType.DMA((dates,)),
            pltpu.SemaphoreType.DMA((OWNERS,)),
        ],
        compiler_params=pltpu.CompilerParams(collective_id=0, has_side_effects=True),
        name="pair_phases",
    )(slc)


def factor_step(block, mat_ref, rhs_ref, low_ref, back_ref, sol_ref):
    base = pl.multiple_of(block * 256, 256)

    def spread(ref, row):
        return jnp.broadcast_to(ref[pl.ds(row, 1), :], (8, LANES))

    s = {}
    for i in range(8):
        for j in range(i, 8):
            s[i, j] = spread(mat_ref, base + i * WIN + j)
    rows = []
    for i in range(8):
        tiles = [mat_ref[pl.ds(pl.multiple_of(base + i * WIN + 8 * t, 8), 8), :] for t in (1, 2, 3)]
        rows.append(tiles + [spread(rhs_ref, block * 8 + i)])
    mult = {}
    inverse = []
    for a in (0, 2, 4, 6):
        b = a + 1
        det = s[a, a] * s[b, b] - s[a, b] * s[a, b]
        scale = 1.0 / det
        e11, e12, e22 = s[b, b] * scale, -s[a, b] * scale, s[a, a] * scale
        inverse.append((e11, e12, e22))
        for i in range(a + 2, 8):
            mult[i, a] = s[a, i] * e11 + s[b, i] * e12
            mult[i, b] = s[a, i] * e12 + s[b, i] * e22
        for i in range(a + 2, 8):
            for j in range(i, 8):
                s[i, j] = s[i, j] - mult[i, a] * s[a, j] - mult[i, b] * s[b, j]
        for i in range(a + 2, 8):
            rows[i] = [rows[i][t] - mult[i, a] * rows[a][t] - mult[i, b] * rows[b][t] for t in range(4)]
    scaled = [None] * 8
    for index, a in enumerate((0, 2, 4, 6)):
        e11, e12, e22 = inverse[index]
        scaled[a] = [e11 * rows[a][t] + e12 * rows[a + 1][t] for t in range(4)]
        scaled[a + 1] = [e12 * rows[a][t] + e22 * rows[a + 1][t] for t in range(4)]
    for k in range(8):
        for t in range(3):
            low_ref[k * 24 + 8 * t:k * 24 + 8 * t + 8, :] = scaled[k][t]
    for r in range(24):
        t = r // 8
        target = pl.multiple_of((block + 1) * 256, 256) + r * WIN
        factors = [jnp.broadcast_to(low_ref[k * 24 + r:k * 24 + r + 1, :], (8, LANES)) for k in range(8)]
        for u in range(t, 3):
            where = pl.ds(pl.multiple_of(target + (u - t) * 8, 8), 8)
            value = mat_ref[where, :]
            for k in range(8):
                value = value - factors[k] * rows[k][u]
            mat_ref[where, :] = value
    for u in range(3):
        where = pl.ds(pl.multiple_of((block + 1 + u) * 8, 8), 8)
        value = rhs_ref[where, :]
        for k in range(8):
            value = value - scaled[k][3] * rows[k][u]
        rhs_ref[where, :] = value
    for a in (6, 4, 2, 0):
        for c in (a, a + 1):
            for i in range(a + 2, 8):
                scaled[c] = [scaled[c][t] - mult[i, c] * scaled[i][t] for t in range(4)]
    sub = lax.broadcasted_iota(jnp.int32, (8, LANES), 0)
    answer = scaled[0][3]
    for i in range(1, 8):
        answer = jnp.where(sub == i, scaled[i][3], answer)
    sol_ref[pl.ds(pl.multiple_of(block * 8, 8), 8), :] = answer
    for i in range(8):
        for t in range(3):
            back_ref[pl.ds((block * 24 + 8 * t) * 9 + i, 8, stride=9), :] = scaled[i][t]


def tree_sum(parts):
    while len(parts) > 1:
        parts = [parts[i] + parts[i + 1] if i + 1 < len(parts) else parts[i]
                 for i in range(0, len(parts), 2)]
    return parts[0]


def back_step(block, back_ref, sol_ref):
    rows = slice(block * 8, block * 8 + 8)

    def product(c):
        start = (block * 24 + c) * 9
        later = jnp.broadcast_to(sol_ref[block * 8 + 8 + c:block * 8 + 9 + c, :], (8, LANES))
        return back_ref[pl.ds(start, 8), :] * later

    value = sol_ref[rows, :] - tree_sum([product(c) for c in range(8, 24)])
    sol_ref[rows, :] = value - tree_sum([product(c) for c in range(8)])


ENDS = 14
LAST = 17


def join_ends(mat_ref, rhs_ref, tmp_ref):
    mine = lax.broadcasted_iota(jnp.int32, (8, LANES), 1) < 8
    for first in range(ENDS, LAST):
        for second in range(first, LAST):
            u = second - first
            for row in range(8):
                start = (first * 8 + row) * WIN + 8 * u
                value = jnp.where(mine, pltpu.roll(mat_ref[start:start + 8, :], LANES - 8, 1), 0.0)
                tmp_ref[pl.ds(7 - row, 8, stride=9), :] = value
            for row in range(8):
                start = ((31 - second) * 8 + row) * WIN + 8 * u
                mat_ref[start:start + 8, :] = mat_ref[start:start + 8, :] + tmp_ref[pl.ds((7 - row) * 9, 8), :]
        value = jnp.where(mine, pltpu.roll(rhs_ref[first * 8:first * 8 + 8, :], LANES - 8, 1), 0.0)
        for row in range(8):
            tmp_ref[80 + 7 - row:80 + 8 - row, :] = value[row:row + 1]
        start = (31 - first) * 8
        rhs_ref[start:start + 8, :] = rhs_ref[start:start + 8, :] + tmp_ref[80:88, :]


def spread_middle(sol_ref, tmp_ref):
    lane = lax.broadcasted_iota(jnp.int32, (8, LANES), 1)
    for block in range(ENDS, LAST + 1):
        value = pltpu.roll(sol_ref[block * 8:block * 8 + 8, :], 8, 1)
        for row in range(8):
            where = (LAST - block) * 8 + 7 - row
            tmp_ref[where:where + 1, :] = value[row:row + 1]
    for block in range(ENDS, LAST + 1):
        other = tmp_ref[(block - ENDS) * 8:(block - ENDS) * 8 + 8, :]
        rows = slice(block * 8, block * 8 + 8)
        sol_ref[rows, :] = jnp.where(lane < 8, sol_ref[rows, :], other)


def solve_kernel(phase_ref, offset_ref, out_ref, live_ref, mat_ref, rhs_ref, low_ref, back_ref, sol_ref, tmp_ref):
    lane = lax.broadcasted_iota(jnp.int32, (8, LANES), 1)
    backwards = LANES - 1 - lane

    def flipped(value):
        return jnp.take_along_axis(value, backwards, axis=1, mode="promise_in_bounds")

    distance = SPAN - lax.broadcasted_iota(jnp.int32, (SPAN, LANES), 0)
    for h in range(2):
        hit = jnp.zeros((SPAN, LANES), F32)
        for k in range(offset_ref.shape[0]):
            entry = jnp.broadcast_to(offset_ref[k:k + 1, h * LANES:(h + 1) * LANES], (SPAN, LANES))
            hit = jnp.where(entry == distance, 1.0, hit)
        live_ref[h] = hit
    sol_ref[...] = jnp.zeros_like(sol_ref)
    blank = jnp.zeros((8, LANES), F32)

    def turned(pairs):
        rows = []
        for low, high in pairs:
            rows += [low, flipped(high)]
        rows += [blank] * (16 - len(rows))
        return jnp.concatenate(rows, axis=0).T

    def current():
        value = sol_ref[0:LANES, :].T
        return [value[:8], flipped(value[8:16])]

    def ahead(pair, shift):
        a, b = (pltpu.roll(v, LANES - shift, 1) for v in pair)
        keep = lane < LANES - shift
        return [jnp.where(keep, a, b), jnp.where(keep, b, a)]

    def behind(pair, shift):
        a, b = (pltpu.roll(v, shift, 1) for v in pair)
        keep = lane >= shift
        return [jnp.where(keep, a, b), jnp.where(keep, b, a)]

    def round_body(_, carry):
        now = current()
        degree = [jnp.full((8, LANES), ridge_weight, F32) for _ in range(2)]
        right = [jnp.zeros((8, LANES), F32) for _ in range(2)]
        zero = jnp.zeros((8, LANES), F32)
        for row in range(LANES):
            mat_ref[row * WIN + 24:row * WIN + 32, :] = zero
        for row in range(LANES, 144):
            for t in range(4):
                mat_ref[row * WIN + 8 * t:row * WIN + 8 * t + 8, :] = zero
        rhs_ref[128:136, :] = zero
        rhs_ref[136:144, :] = zero

        stack = []
        for d in range(1, SPAN + 1):
            later = ahead(now, d)
            weights, moments = [], []
            for h in range(2):
                phase = phase_ref[h, pl.ds(SPAN - d, 8, stride=WIN), :]
                residual = phase - (now[h] - later[h])
                live = jnp.broadcast_to(live_ref[h, SPAN - d:SPAN - d + 1, :], (8, LANES))
                weight = live / jnp.maximum(jnp.abs(residual), floor_value)
                weights.append(weight)
                moments.append(weight * phase)
            from_w, from_m = behind(weights, d), behind(moments, d)
            for h in range(2):
                degree[h] = degree[h] + (weights[h] + from_w[h])
                right[h] = right[h] + (moments[h] - from_m[h])
            crossing = jnp.where(lane < min(d, 16), 0.0, from_w[1])
            stack.append((-weights[0], -crossing))
            if len(stack) == 8:
                columns = turned(stack)
                for e in range(8):
                    column = columns if e == 0 else pltpu.roll(columns, LANES - 16 * e, 1)
                    for b in range(16):
                        where = pl.ds(b * 256 + d - 7 + e, 8, stride=WIN + 1)
                        mat_ref[where, :] = column[b * 8:b * 8 + 8]
                stack = []
        columns = turned([degree, right])
        for b in range(16):
            mat_ref[pl.ds(b * 256, 8, stride=WIN + 1), :] = columns[b * 8:b * 8 + 8]
        rhs_ref[0:LANES, :] = pltpu.roll(columns, LANES - 16, 1)

        def forward(i, c):
            factor_step(i, mat_ref, rhs_ref, low_ref, back_ref, sol_ref)
            return c

        lax.fori_loop(0, ENDS, forward, 0)
        join_ends(mat_ref, rhs_ref, tmp_ref)
        lax.fori_loop(ENDS, LAST + 1, forward, 0)

        for block in range(LAST, ENDS - 1, -1):
            back_step(block, back_ref, sol_ref)
        spread_middle(sol_ref, tmp_ref)
        for block in range(ENDS - 1, -1, -1):
            back_step(block, back_ref, sol_ref)
        return carry

    lax.fori_loop(0, ITERS, round_body, 0)
    now = current()
    for h in range(2):
        out_ref[:, h * LANES:(h + 1) * LANES] = now[h]


def solve(phases, offsets):
    return pl.pallas_call(
        solve_kernel,
        out_shape=jax.ShapeDtypeStruct((8, 256), F32),
        in_specs=[pl.BlockSpec(memory_space=pltpu.VMEM)] * 2,
        out_specs=pl.BlockSpec(memory_space=pltpu.VMEM),
        scratch_shapes=[
            pltpu.VMEM((2, SPAN, LANES), F32),
            pltpu.VMEM((168 * WIN, LANES), F32),
            pltpu.VMEM((168, LANES), F32),
            pltpu.VMEM((8 * 24, LANES), F32),
            pltpu.VMEM((18 * 24 * 9, LANES), F32),
            pltpu.VMEM((168, LANES), F32),
            pltpu.VMEM((96, LANES), F32),
        ],
        name="solve",
    )(phases, offsets)


def local(slc, offsets):
    rows_first = jnp.transpose(slc, (0, 2, 1, 3))
    phases = pair_phases(rows_first, lax.axis_size("date"), lax.axis_size("tile"))
    series = solve(phases, offsets.T)
    return series.T[:, None, :]


def solution(mesh):
    return jax.shard_map(
        local,
        mesh=mesh,
        in_specs=(P(None, "date", None, "tile"), P()),
        out_specs=P(None, "tile", "date"),
        check_vma=False,
    )
```

```python
import jax
import jax.numpy as jnp
from jax import lax
from jax.experimental import pallas as pl
from jax.experimental.pallas import tpu as pltpu
from jax.sharding import PartitionSpec as P

LOOK_AZ = 5
LOOK_RG = 20
SPAN = 24
ITERS = 2
LANES = 128
WIN = 32

floor_value = 0.05
ridge_weight = 1.0
F32 = jnp.float32
MESH = pl.DeviceIdType.MESH
OWNERS = 12
OWNER_STEP = 5
OWNER_INVERSE = 13
RING = 4


def gather_step(step, slc_ref, send_ref):
    lane = lax.broadcasted_iota(jnp.int32, (16, LANES), 1)
    half = step // 4
    quarter = step % 4
    blank = jnp.zeros((16, LANES), F32)
    moved = []
    for rho in range(LOOK_AZ):
        amount = LOOK_RG * rho
        line = []
        for t in range(5):
            columns = pl.ds(pl.multiple_of((quarter * 5 + t) * LANES, LANES), LANES)
            row = half * LOOK_AZ + rho
            line.append(jnp.concatenate([
                slc_ref[0, row, :, columns].astype(F32),
                slc_ref[1, row, :, columns].astype(F32),
            ], axis=0))
        if amount == 0:
            moved.append(line + [blank])
            continue
        rolled = [blank] + [pltpu.roll(v, amount, 1) for v in line] + [blank]
        moved.append([jnp.where(lane < amount, rolled[t], rolled[t + 1]) for t in range(6)])
    for local_pixel in range(32):
        start = LOOK_RG * local_pixel
        tile, offset = start // LANES, start % LANES
        out = blank
        for rho in range(LOOK_AZ):
            lo = offset + LOOK_RG * rho
            hi = lo + LOOK_RG
            if lo < LANES:
                out = jnp.where((lane >= lo) & (lane < hi), moved[rho][tile], out)
            if hi > LANES:
                mask = (lane >= lo - LANES) & (lane < hi - LANES)
                out = jnp.where(mask, moved[rho][tile + 1], out)
        slot = half * 16 + quarter * 4 + local_pixel // 8
        send_ref[slot, local_pixel % 8] = out.astype(jnp.bfloat16)


def skewed(gram_ref, index, block, place):
    rows = pl.ds(block * 8, 8)
    first = gram_ref[index + (rows, pl.ds(0, LANES))] if block >= 13 else None
    second = gram_ref[index + (rows, pl.ds(LANES, LANES))] if block < 16 else None
    if first is None:
        value = second
    elif second is None:
        value = first
    else:
        lane = lax.broadcasted_iota(jnp.int32, (8, LANES), 1)
        value = jnp.where(lane >= 64, first, second)
    shift = (place * WIN + SPAN + 1 + block * 8) % LANES
    return pltpu.roll(value, shift, 1, stride=1, stride_axis=0)


def front_kernel(slc_hbm, phase_ref, slc_ref, send_ref, recv_ref, gram_ref, total_ref, band_ref,
                 part_ref, gathered_ref, anchor_ref, load_sem, send_sem, recv_sem, part_send,
                 part_recv, column_send, column_recv, plane_send, plane_recv):
    dates = send_ref.shape[0]
    tiles = lax.axis_size("tile")
    me = lax.axis_index("date")
    tile = lax.axis_index("tile")
    middle = tiles // 2
    lane = lax.broadcasted_iota(jnp.int32, (8, LANES), 1)
    load = pltpu.make_async_copy(slc_hbm, slc_ref, load_sem)
    load.start()

    def peer(k):
        return me ^ (dates - 1 - k)

    def for_peers(action):
        def go(k, carry):
            action(peer(k))
            return carry

        lax.fori_loop(0, dates - 1, go, 0, unroll=True)

    def for_far_peers(action):
        steps = [(dx, dy, dc) for dx in range(RING) for dy in range(RING) for dc in range(2)]
        steps.sort(key=lambda v: -(min(v[0], RING - v[0]) + min(v[1], RING - v[1]) + v[2] / 4))
        for dx, dy, dc in steps[:-1]:
            across = (me // (2 * RING) + dx) % RING
            along = (me // 2 + dy) % RING
            core = (me + dc) % 2
            action((across * RING + along) * 2 + core)

    def for_column(action):
        def go(k, carry):
            action(lax.rem(tile + k, tiles))
            return carry

        lax.fori_loop(1, tiles, go, 0)

    barrier = pltpu.get_barrier_semaphore()
    for_column(lambda other: pl.semaphore_signal(
        barrier, inc=1, device_id={"tile": other}, device_id_type=MESH))
    for_peers(lambda other: pl.semaphore_signal(
        barrier, inc=1, device_id={"date": other}, device_id_type=MESH))
    load.wait()

    def sample_copy(other, slot):
        return pltpu.make_async_remote_copy(
            src_ref=send_ref.at[other], dst_ref=recv_ref.at[slot],
            send_sem=send_sem.at[other], recv_sem=recv_sem.at[slot],
            device_id={"date": other}, device_id_type=MESH)

    def gather(step, carry):
        gather_step(step, slc_ref, send_ref)
        return carry

    lax.fori_loop(0, 8, gather, 0)
    pl.semaphore_wait(barrier, dates - 1 + tiles - 1)
    for_far_peers(lambda other: sample_copy(other, me).start())
    recv_ref[me] = send_ref[me]

    row_id = lax.broadcasted_iota(jnp.int32, (256, 256), 0)
    col_id = lax.broadcasted_iota(jnp.int32, (256, 256), 1)
    mirror = (row_id + col_id == 255).astype(F32).astype(jnp.bfloat16)
    contract = (((1,), (1,)), ((), ()))

    for_peers(lambda other: sample_copy(other, other).wait_recv())
    for pixel in range(8):
        both = recv_ref[:, pixel].astype(F32)
        real = both[:, :8].reshape(256, LANES)
        imag = both[:, 8:].reshape(256, LANES)
        right = jnp.concatenate([real, imag], axis=1).astype(jnp.bfloat16)
        turned = jnp.concatenate([imag, -real], axis=1).astype(jnp.bfloat16)
        descending = jnp.dot(mirror, right, preferred_element_type=F32).astype(jnp.bfloat16)
        for part, left in enumerate((right, turned)):
            gram = lax.dot_general(left, descending, contract, preferred_element_type=F32)
            gram_ref[pixel, part] = gram
            if pixel == 0:
                total_ref[part] = gram
            else:
                total_ref[part] = total_ref[part] + gram

    def owner_date(owner):
        return lax.rem(owner * OWNER_STEP, dates)

    owned = lax.rem(me * OWNER_INVERSE, dates)

    def part_copy(owner, slot):
        return pltpu.make_async_remote_copy(
            src_ref=part_ref.at[owner], dst_ref=gathered_ref.at[slot],
            send_sem=part_send.at[owner], recv_sem=part_recv.at[slot],
            device_id={"date": owner_date(owner)}, device_id_type=MESH)

    def for_owners(action):
        def go(owner, carry):
            @pl.when(owner != owned)
            def _():
                action(owner)

            return carry

        lax.fori_loop(0, OWNERS, go, 0, unroll=True)

    @pl.when(tile == middle)
    def _():
        for block in range(32):
            value = jnp.where(lane < WIN, skewed(total_ref, (0,), block, 0), skewed(total_ref, (1,), block, 1))
            band_ref[0, 0, block * 8:block * 8 + 8, :] = value
        for half in range(2):
            turned = band_ref[0, 0, half * LANES:(half + 1) * LANES, :].T
            for sixth in range(6):
                owner = half * 6 + sixth
                part_ref[owner, 0:4, :] = turned[sixth * 4:sixth * 4 + 4]
                part_ref[owner, 4:8, :] = turned[WIN + sixth * 4:WIN + sixth * 4 + 4]
        for_owners(lambda owner: part_copy(owner, me).start())

    def bands(group, carry):
        for part in range(2):
            for block in range(32):
                value = skewed(gram_ref, (group * 4, part), block, 0)
                for place in range(1, 4):
                    other = skewed(gram_ref, (group * 4 + place, part), block, place)
                    value = jnp.where(lane < place * WIN, value, other)
                band_ref[part, group, block * 8:block * 8 + 8, :] = value
        for half in range(2):
            rows = slice(half * LANES, (half + 1) * LANES)
            real = band_ref[0, group, rows, :].T
            imag = band_ref[1, group, rows, :].T
            phase_ref[half, pl.ds(pl.multiple_of(group * LANES, LANES), LANES), :] = jnp.arctan2(imag, real)
        return carry

    lax.fori_loop(0, 2, bands, 0)

    def column_copy(owner, other):
        return pltpu.make_async_remote_copy(
            src_ref=anchor_ref.at[owner], dst_ref=anchor_ref.at[owner],
            send_sem=column_send.at[other], recv_sem=column_recv.at[0],
            device_id={"tile": other}, device_id_type=MESH)

    def plane_copy(owner, other):
        return pltpu.make_async_remote_copy(
            src_ref=anchor_ref.at[owner], dst_ref=anchor_ref.at[owner],
            send_sem=plane_send.at[other], recv_sem=plane_recv.at[owner],
            device_id={"date": other}, device_id_type=MESH)

    @pl.when((owned < OWNERS) & (tile == middle))
    def _():
        def part_arrive(k, total):
            other = peer(k)
            part_copy(owned, other).wait_recv()
            return total + gathered_ref[other]

        total = lax.fori_loop(0, dates - 1, part_arrive, part_ref[owned])
        anchor_ref[owned] = jnp.arctan2(total[4:], total[:4])
        for_column(lambda other: column_copy(owned, other).start())

    @pl.when((owned < OWNERS) & (tile != middle))
    def _():
        column_copy(owned, middle).wait_recv()

    @pl.when(owned < OWNERS)
    def _():
        for_far_peers(lambda other: plane_copy(owned, other).start())

    for_peers(lambda other: sample_copy(other, me).wait_send())

    @pl.when(tile == middle)
    def _():
        for_owners(lambda owner: part_copy(owner, me).wait_send())

    for_owners(lambda owner: plane_copy(owner, owner_date(owner)).wait_recv())

    for half in range(2):
        base = jnp.concatenate([anchor_ref[half * 6 + t] for t in range(6)], axis=0)
        for pixel in range(8):
            rows = slice(pixel * WIN, pixel * WIN + SPAN)
            phase_ref[half, rows, :] = phase_ref[half, rows, :] - base

    @pl.when(owned < OWNERS)
    def _():
        for_peers(lambda other: plane_copy(owned, other).wait_send())

    @pl.when((owned < OWNERS) & (tile == middle))
    def _():
        for_column(lambda other: column_copy(owned, other).wait_send())


def pair_phases(slc, dates, tiles):
    return pl.pallas_call(
        front_kernel,
        out_shape=jax.ShapeDtypeStruct((2, 256, LANES), F32),
        in_specs=[pl.BlockSpec(memory_space=pl.ANY)],
        out_specs=pl.BlockSpec(memory_space=pltpu.VMEM),
        scratch_shapes=[
            pltpu.VMEM(slc.shape, slc.dtype),
            pltpu.VMEM((dates, 8, 16, LANES), jnp.bfloat16),
            pltpu.VMEM((dates, 8, 16, LANES), jnp.bfloat16),
            pltpu.VMEM((8, 2, 256, 256), F32),
            pltpu.VMEM((2, 256, 256), F32),
            pltpu.VMEM((2, 2, 256, LANES), F32),
            pltpu.VMEM((OWNERS, 8, LANES), F32),
            pltpu.VMEM((dates, 8, LANES), F32),
            pltpu.VMEM((OWNERS, 4, LANES), F32),
            pltpu.SemaphoreType.DMA(()),
            pltpu.SemaphoreType.DMA((dates,)),
            pltpu.SemaphoreType.DMA((dates,)),
            pltpu.SemaphoreType.DMA((OWNERS,)),
            pltpu.SemaphoreType.DMA((dates,)),
            pltpu.SemaphoreType.DMA((tiles,)),
            pltpu.SemaphoreType.DMA((1,)),
            pltpu.SemaphoreType.DMA((dates,)),
            pltpu.SemaphoreType.DMA((OWNERS,)),
        ],
        compiler_params=pltpu.CompilerParams(collective_id=0, has_side_effects=True),
        name="pair_phases",
    )(slc)


def aligned(value, unit):
    return value if isinstance(value, int) else pl.multiple_of(value, unit)


def factor_step(block, mat_ref, rhs_ref, low_ref, back_ref, sol_ref, tiles=3):
    base = aligned(block * 256, 256)

    def spread(ref, row):
        return jnp.broadcast_to(ref[pl.ds(row, 1), :], (8, LANES))

    s = {}
    for i in range(8):
        for j in range(i, 8):
            s[i, j] = spread(mat_ref, base + i * WIN + j)
    rows = []
    for i in range(8):
        later = [mat_ref[pl.ds(aligned(base + i * WIN + 8 * t, 8), 8), :] for t in range(1, tiles + 1)]
        rows.append(later + [spread(rhs_ref, block * 8 + i)])
    mult = {}
    inverse = []
    for a in (0, 2, 4, 6):
        b = a + 1
        det = s[a, a] * s[b, b] - s[a, b] * s[a, b]
        scale = 1.0 / det
        e11, e12, e22 = s[b, b] * scale, -s[a, b] * scale, s[a, a] * scale
        inverse.append((e11, e12, e22))
        for i in range(a + 2, 8):
            mult[i, a] = s[a, i] * e11 + s[b, i] * e12
            mult[i, b] = s[a, i] * e12 + s[b, i] * e22
        for i in range(a + 2, 8):
            for j in range(i, 8):
                s[i, j] = s[i, j] - mult[i, a] * s[a, j] - mult[i, b] * s[b, j]
        for i in range(a + 2, 8):
            rows[i] = [rows[i][t] - mult[i, a] * rows[a][t] - mult[i, b] * rows[b][t] for t in range(tiles + 1)]
    scaled = [None] * 8
    for index, a in enumerate((0, 2, 4, 6)):
        e11, e12, e22 = inverse[index]
        scaled[a] = [e11 * rows[a][t] + e12 * rows[a + 1][t] for t in range(tiles + 1)]
        scaled[a + 1] = [e12 * rows[a][t] + e22 * rows[a + 1][t] for t in range(tiles + 1)]
    for k in range(8):
        for t in range(tiles):
            low_ref[k * 24 + 8 * t:k * 24 + 8 * t + 8, :] = scaled[k][t]
    for r in range(8 * tiles):
        t = r // 8
        target = aligned((block + 1) * 256, 256) + r * WIN
        first = max(r - 16, 0) // 2 * 2
        factors = {k: jnp.broadcast_to(low_ref[k * 24 + r:k * 24 + r + 1, :], (8, LANES))
                   for k in range(first, 8)}
        for u in range(t, tiles):
            where = pl.ds(aligned(target + (u - t) * 8, 8), 8)
            value = mat_ref[where, :]
            for k in range(first, 8):
                value = value - factors[k] * rows[k][u]
            mat_ref[where, :] = value
    for u in range(tiles):
        where = pl.ds(aligned((block + 1 + u) * 8, 8), 8)
        value = rhs_ref[where, :]
        for k in range(8):
            value = value - scaled[k][tiles] * rows[k][u]
        rhs_ref[where, :] = value
    for a in (6, 4, 2, 0):
        for c in (a, a + 1):
            for i in range(a + 2, 8):
                scaled[c] = [scaled[c][t] - mult[i, c] * scaled[i][t] for t in range(tiles + 1)]
    sub = lax.broadcasted_iota(jnp.int32, (8, LANES), 0)
    answer = scaled[0][tiles]
    for i in range(1, 8):
        answer = jnp.where(sub == i, scaled[i][tiles], answer)
    sol_ref[pl.ds(aligned(block * 8, 8), 8), :] = answer
    for i in range(8):
        for t in range(tiles):
            back_ref[pl.ds((block * 24 + 8 * t) * 9 + i, 8, stride=9), :] = scaled[i][t]


def tree_sum(parts):
    while len(parts) > 1:
        parts = [parts[i] + parts[i + 1] if i + 1 < len(parts) else parts[i]
                 for i in range(0, len(parts), 2)]
    return parts[0]


def back_step(block, back_ref, sol_ref, tiles=3):
    rows = slice(block * 8, block * 8 + 8)

    def product(c):
        start = (block * 24 + c) * 9
        later = jnp.broadcast_to(sol_ref[block * 8 + 8 + c:block * 8 + 9 + c, :], (8, LANES))
        return back_ref[pl.ds(start, 8), :] * later

    value = sol_ref[rows, :]
    if tiles > 1:
        value = value - tree_sum([product(c) for c in range(8, 8 * tiles)])
    if tiles > 0:
        sol_ref[rows, :] = value - tree_sum([product(c) for c in range(8)])


ENDS = 14
LAST = 17


def join_ends(mat_ref, rhs_ref, tmp_ref):
    mine = lax.broadcasted_iota(jnp.int32, (8, LANES), 1) < 8
    for first in range(ENDS, LAST):
        for second in range(first, LAST):
            u = second - first
            for row in range(8):
                start = (first * 8 + row) * WIN + 8 * u
                value = jnp.where(mine, pltpu.roll(mat_ref[start:start + 8, :], LANES - 8, 1), 0.0)
                tmp_ref[pl.ds(7 - row, 8, stride=9), :] = value
            for row in range(8):
                start = ((31 - second) * 8 + row) * WIN + 8 * u
                mat_ref[start:start + 8, :] = mat_ref[start:start + 8, :] + tmp_ref[pl.ds((7 - row) * 9, 8), :]
        value = jnp.where(mine, pltpu.roll(rhs_ref[first * 8:first * 8 + 8, :], LANES - 8, 1), 0.0)
        for row in range(8):
            tmp_ref[80 + 7 - row:80 + 8 - row, :] = value[row:row + 1]
        start = (31 - first) * 8
        rhs_ref[start:start + 8, :] = rhs_ref[start:start + 8, :] + tmp_ref[80:88, :]


def spread_middle(sol_ref, tmp_ref):
    lane = lax.broadcasted_iota(jnp.int32, (8, LANES), 1)
    for block in range(ENDS, LAST + 1):
        value = pltpu.roll(sol_ref[block * 8:block * 8 + 8, :], 8, 1)
        for row in range(8):
            where = (LAST - block) * 8 + 7 - row
            tmp_ref[where:where + 1, :] = value[row:row + 1]
    for block in range(ENDS, LAST + 1):
        other = tmp_ref[(block - ENDS) * 8:(block - ENDS) * 8 + 8, :]
        rows = slice(block * 8, block * 8 + 8)
        sol_ref[rows, :] = jnp.where(lane < 8, sol_ref[rows, :], other)


def solve_kernel(phase_ref, offset_ref, out_ref, live_ref, mat_ref, rhs_ref, low_ref, back_ref, sol_ref, tmp_ref):
    lane = lax.broadcasted_iota(jnp.int32, (8, LANES), 1)
    backwards = LANES - 1 - lane

    def flipped(value):
        return jnp.take_along_axis(value, backwards, axis=1, mode="promise_in_bounds")

    distance = SPAN - lax.broadcasted_iota(jnp.int32, (SPAN, LANES), 0)
    for h in range(2):
        hit = jnp.zeros((SPAN, LANES), F32)
        for k in range(offset_ref.shape[0]):
            entry = jnp.broadcast_to(offset_ref[k:k + 1, h * LANES:(h + 1) * LANES], (SPAN, LANES))
            hit = jnp.where(entry == distance, 1.0, hit)
        live_ref[h] = hit
    sol_ref[...] = jnp.zeros_like(sol_ref)
    blank = jnp.zeros((8, LANES), F32)

    def turned(pairs):
        rows = []
        for low, high in pairs:
            rows += [low, flipped(high)]
        rows += [blank] * (16 - len(rows))
        return jnp.concatenate(rows, axis=0).T

    def current():
        value = sol_ref[0:LANES, :].T
        return [value[:8], flipped(value[8:16])]

    def ahead(pair, shift):
        a, b = (pltpu.roll(v, LANES - shift, 1) for v in pair)
        keep = lane < LANES - shift
        return [jnp.where(keep, a, b), jnp.where(keep, b, a)]

    def behind(pair, shift):
        a, b = (pltpu.roll(v, shift, 1) for v in pair)
        keep = lane >= shift
        return [jnp.where(keep, a, b), jnp.where(keep, b, a)]

    def round_body(_, carry):
        now = current()
        degree = [jnp.full((8, LANES), ridge_weight, F32) for _ in range(2)]
        right = [jnp.zeros((8, LANES), F32) for _ in range(2)]
        zero = jnp.zeros((8, LANES), F32)
        for row in range(LANES):
            mat_ref[row * WIN + 24:row * WIN + 32, :] = zero
        for row in range(LANES, 144):
            for t in range(4):
                mat_ref[row * WIN + 8 * t:row * WIN + 8 * t + 8, :] = zero
        rhs_ref[128:136, :] = zero
        rhs_ref[136:144, :] = zero

        stack = []
        for d in range(1, SPAN + 1):
            later = ahead(now, d)
            weights, moments = [], []
            for h in range(2):
                phase = phase_ref[h, pl.ds(SPAN - d, 8, stride=WIN), :]
                residual = phase - (now[h] - later[h])
                live = jnp.broadcast_to(live_ref[h, SPAN - d:SPAN - d + 1, :], (8, LANES))
                weight = live / jnp.maximum(jnp.abs(residual), floor_value)
                weights.append(weight)
                moments.append(weight * phase)
            from_w, from_m = behind(weights, d), behind(moments, d)
            for h in range(2):
                degree[h] = degree[h] + (weights[h] + from_w[h])
                right[h] = right[h] + (moments[h] - from_m[h])
            crossing = jnp.where(lane < min(d, 16), 0.0, from_w[1])
            stack.append((-weights[0], -crossing))
            if len(stack) == 8:
                columns = turned(stack)
                for e in range(8):
                    column = columns if e == 0 else pltpu.roll(columns, LANES - 16 * e, 1)
                    for b in range(16):
                        where = pl.ds(b * 256 + d - 7 + e, 8, stride=WIN + 1)
                        mat_ref[where, :] = column[b * 8:b * 8 + 8]
                stack = []
        columns = turned([degree, right])
        for b in range(16):
            mat_ref[pl.ds(b * 256, 8, stride=WIN + 1), :] = columns[b * 8:b * 8 + 8]
        rhs_ref[0:LANES, :] = pltpu.roll(columns, LANES - 16, 1)

        def forward(i, c):
            factor_step(i, mat_ref, rhs_ref, low_ref, back_ref, sol_ref)
            return c

        lax.fori_loop(0, ENDS, forward, 0, unroll=2)
        join_ends(mat_ref, rhs_ref, tmp_ref)
        for block in range(ENDS, LAST + 1):
            factor_step(block, mat_ref, rhs_ref, low_ref, back_ref, sol_ref, LAST - block)

        for block in range(LAST, ENDS - 1, -1):
            back_step(block, back_ref, sol_ref, LAST - block)
        spread_middle(sol_ref, tmp_ref)
        for block in range(ENDS - 1, -1, -1):
            back_step(block, back_ref, sol_ref)
        return carry

    lax.fori_loop(0, ITERS, round_body, 0)
    now = current()
    for h in range(2):
        out_ref[:, h * LANES:(h + 1) * LANES] = now[h]


def solve(phases, offsets):
    return pl.pallas_call(
        solve_kernel,
        out_shape=jax.ShapeDtypeStruct((8, 256), F32),
        in_specs=[pl.BlockSpec(memory_space=pltpu.VMEM)] * 2,
        out_specs=pl.BlockSpec(memory_space=pltpu.VMEM),
        scratch_shapes=[
            pltpu.VMEM((2, SPAN, LANES), F32),
            pltpu.VMEM((168 * WIN, LANES), F32),
            pltpu.VMEM((168, LANES), F32),
            pltpu.VMEM((8 * 24, LANES), F32),
            pltpu.VMEM((18 * 24 * 9, LANES), F32),
            pltpu.VMEM((168, LANES), F32),
            pltpu.VMEM((96, LANES), F32),
        ],
        name="solve",
    )(phases, offsets)


def local(slc, offsets):
    rows_first = jnp.transpose(slc, (0, 2, 1, 3))
    phases = pair_phases(rows_first, lax.axis_size("date"), lax.axis_size("tile"))
    series = solve(phases, offsets.T)
    return series.T[:, None, :]


def solution(mesh):
    return jax.shard_map(
        local,
        mesh=mesh,
        in_specs=(P(None, "date", None, "tile"), P()),
        out_specs=P(None, "tile", "date"),
        check_vma=False,
    )
```

```python
import jax
import jax.numpy as jnp
from jax import lax
from jax.experimental import pallas as pl
from jax.experimental.pallas import tpu as pltpu
from jax.sharding import PartitionSpec as P

LOOK_AZ = 5
LOOK_RG = 20
SPAN = 24
ITERS = 2
LANES = 128
WIN = 32

floor_value = 0.05
ridge_weight = 1.0
F32 = jnp.float32
MESH = pl.DeviceIdType.MESH
OWNERS = 12
OWNER_STEP = 5
OWNER_INVERSE = 13
RING = 4


def gather_step(step, slc_ref, send_ref):
    lane = lax.broadcasted_iota(jnp.int32, (16, LANES), 1)
    half = step // 4
    quarter = step % 4
    blank = jnp.zeros((16, LANES), F32)
    moved = []
    for rho in range(LOOK_AZ):
        amount = LOOK_RG * rho
        line = []
        for t in range(5):
            columns = pl.ds(pl.multiple_of((quarter * 5 + t) * LANES, LANES), LANES)
            row = half * LOOK_AZ + rho
            line.append(jnp.concatenate([
                slc_ref[0, row, :, columns].astype(F32),
                slc_ref[1, row, :, columns].astype(F32),
            ], axis=0))
        if amount == 0:
            moved.append(line + [blank])
            continue
        rolled = [blank] + [pltpu.roll(v, amount, 1) for v in line] + [blank]
        moved.append([jnp.where(lane < amount, rolled[t], rolled[t + 1]) for t in range(6)])
    for local_pixel in range(32):
        start = LOOK_RG * local_pixel
        tile, offset = start // LANES, start % LANES
        out = blank
        for rho in range(LOOK_AZ):
            lo = offset + LOOK_RG * rho
            hi = lo + LOOK_RG
            if lo < LANES:
                out = jnp.where((lane >= lo) & (lane < hi), moved[rho][tile], out)
            if hi > LANES:
                mask = (lane >= lo - LANES) & (lane < hi - LANES)
                out = jnp.where(mask, moved[rho][tile + 1], out)
        slot = half * 16 + quarter * 4 + local_pixel // 8
        send_ref[slot, local_pixel % 8] = out.astype(jnp.bfloat16)


def skewed(gram_ref, index, block, place):
    rows = pl.ds(block * 8, 8)
    first = gram_ref[index + (rows, pl.ds(0, LANES))] if block >= 13 else None
    second = gram_ref[index + (rows, pl.ds(LANES, LANES))] if block < 16 else None
    if first is None:
        value = second
    elif second is None:
        value = first
    else:
        lane = lax.broadcasted_iota(jnp.int32, (8, LANES), 1)
        value = jnp.where(lane >= 64, first, second)
    shift = (place * WIN + SPAN + 1 + block * 8) % LANES
    return pltpu.roll(value, shift, 1, stride=1, stride_axis=0)


def front_kernel(slc_hbm, phase_ref, slc_ref, send_ref, recv_ref, gram_ref, total_ref, band_ref,
                 part_ref, gathered_ref, anchor_ref, load_sem, send_sem, recv_sem, part_send,
                 part_recv, column_send, column_recv, plane_send, plane_recv):
    dates = send_ref.shape[0]
    tiles = lax.axis_size("tile")
    me = lax.axis_index("date")
    tile = lax.axis_index("tile")
    middle = tiles // 2
    lane = lax.broadcasted_iota(jnp.int32, (8, LANES), 1)
    load = pltpu.make_async_copy(slc_hbm, slc_ref, load_sem)
    load.start()

    def peer(k):
        return me ^ (dates - 1 - k)

    def for_peers(action):
        def go(k, carry):
            action(peer(k))
            return carry

        lax.fori_loop(0, dates - 1, go, 0, unroll=True)

    def for_far_peers(action):
        steps = [(dx, dy, dc) for dx in range(RING) for dy in range(RING) for dc in range(2)]
        steps.sort(key=lambda v: -(min(v[0], RING - v[0]) + min(v[1], RING - v[1]) + v[2] / 4))
        for dx, dy, dc in steps[:-1]:
            across = (me // (2 * RING) + dx) % RING
            along = (me // 2 + dy) % RING
            core = (me + dc) % 2
            action((across * RING + along) * 2 + core)

    def for_column(action):
        def go(k, carry):
            action(lax.rem(tile + k, tiles))
            return carry

        lax.fori_loop(1, tiles, go, 0)

    barrier = pltpu.get_barrier_semaphore()
    for_column(lambda other: pl.semaphore_signal(
        barrier, inc=1, device_id={"tile": other}, device_id_type=MESH))
    for_peers(lambda other: pl.semaphore_signal(
        barrier, inc=1, device_id={"date": other}, device_id_type=MESH))
    load.wait()

    def sample_copy(other, slot):
        return pltpu.make_async_remote_copy(
            src_ref=send_ref.at[other], dst_ref=recv_ref.at[slot],
            send_sem=send_sem.at[other], recv_sem=recv_sem.at[slot],
            device_id={"date": other}, device_id_type=MESH)

    def gather(step, carry):
        gather_step(step, slc_ref, send_ref)
        return carry

    lax.fori_loop(0, 8, gather, 0)
    pl.semaphore_wait(barrier, dates - 1 + tiles - 1)
    for_far_peers(lambda other: sample_copy(other, me).start())
    recv_ref[me] = send_ref[me]

    row_id = lax.broadcasted_iota(jnp.int32, (256, 256), 0)
    col_id = lax.broadcasted_iota(jnp.int32, (256, 256), 1)
    mirror = (row_id + col_id == 255).astype(F32).astype(jnp.bfloat16)
    contract = (((1,), (1,)), ((), ()))

    for_peers(lambda other: sample_copy(other, other).wait_recv())
    for pixel in range(8):
        both = recv_ref[:, pixel].astype(F32)
        real = both[:, :8].reshape(256, LANES)
        imag = both[:, 8:].reshape(256, LANES)
        right = jnp.concatenate([real, imag], axis=1).astype(jnp.bfloat16)
        turned = jnp.concatenate([imag, -real], axis=1).astype(jnp.bfloat16)
        descending = jnp.dot(mirror, right, preferred_element_type=F32).astype(jnp.bfloat16)
        for part, left in enumerate((right, turned)):
            gram = lax.dot_general(left, descending, contract, preferred_element_type=F32)
            gram_ref[pixel, part] = gram
            if pixel == 0:
                total_ref[part] = gram
            else:
                total_ref[part] = total_ref[part] + gram

    def owner_date(owner):
        return lax.rem(owner * OWNER_STEP, dates)

    owned = lax.rem(me * OWNER_INVERSE, dates)

    def part_copy(owner, slot):
        return pltpu.make_async_remote_copy(
            src_ref=part_ref.at[owner], dst_ref=gathered_ref.at[slot],
            send_sem=part_send.at[owner], recv_sem=part_recv.at[slot],
            device_id={"date": owner_date(owner)}, device_id_type=MESH)

    def for_owners(action):
        def go(owner, carry):
            @pl.when(owner != owned)
            def _():
                action(owner)

            return carry

        lax.fori_loop(0, OWNERS, go, 0, unroll=True)

    @pl.when(tile == middle)
    def _():
        for block in range(32):
            value = jnp.where(lane < WIN, skewed(total_ref, (0,), block, 0), skewed(total_ref, (1,), block, 1))
            band_ref[0, 0, block * 8:block * 8 + 8, :] = value
        for half in range(2):
            turned = band_ref[0, 0, half * LANES:(half + 1) * LANES, :].T
            for sixth in range(6):
                owner = half * 6 + sixth
                part_ref[owner, 0:4, :] = turned[sixth * 4:sixth * 4 + 4]
                part_ref[owner, 4:8, :] = turned[WIN + sixth * 4:WIN + sixth * 4 + 4]
        for_owners(lambda owner: part_copy(owner, me).start())

    def bands(group, carry):
        for part in range(2):
            for block in range(32):
                value = skewed(gram_ref, (group * 4, part), block, 0)
                for place in range(1, 4):
                    other = skewed(gram_ref, (group * 4 + place, part), block, place)
                    value = jnp.where(lane < place * WIN, value, other)
                band_ref[part, group, block * 8:block * 8 + 8, :] = value
        for half in range(2):
            rows = slice(half * LANES, (half + 1) * LANES)
            real = band_ref[0, group, rows, :].T
            imag = band_ref[1, group, rows, :].T
            phase_ref[half, pl.ds(pl.multiple_of(group * LANES, LANES), LANES), :] = jnp.arctan2(imag, real)
        return carry

    lax.fori_loop(0, 2, bands, 0)

    def column_copy(owner, other):
        return pltpu.make_async_remote_copy(
            src_ref=anchor_ref.at[owner], dst_ref=anchor_ref.at[owner],
            send_sem=column_send.at[other], recv_sem=column_recv.at[0],
            device_id={"tile": other}, device_id_type=MESH)

    def plane_copy(owner, other):
        return pltpu.make_async_remote_copy(
            src_ref=anchor_ref.at[owner], dst_ref=anchor_ref.at[owner],
            send_sem=plane_send.at[other], recv_sem=plane_recv.at[owner],
            device_id={"date": other}, device_id_type=MESH)

    @pl.when((owned < OWNERS) & (tile == middle))
    def _():
        def part_arrive(k, total):
            other = peer(k)
            part_copy(owned, other).wait_recv()
            return total + gathered_ref[other]

        total = lax.fori_loop(0, dates - 1, part_arrive, part_ref[owned])
        anchor_ref[owned] = jnp.arctan2(total[4:], total[:4])
        for_column(lambda other: column_copy(owned, other).start())

    @pl.when((owned < OWNERS) & (tile != middle))
    def _():
        column_copy(owned, middle).wait_recv()

    @pl.when(owned < OWNERS)
    def _():
        for_far_peers(lambda other: plane_copy(owned, other).start())

    for_peers(lambda other: sample_copy(other, me).wait_send())

    @pl.when(tile == middle)
    def _():
        for_owners(lambda owner: part_copy(owner, me).wait_send())

    for_owners(lambda owner: plane_copy(owner, owner_date(owner)).wait_recv())

    for half in range(2):
        base = jnp.concatenate([anchor_ref[half * 6 + t] for t in range(6)], axis=0)
        for pixel in range(8):
            rows = slice(pixel * WIN, pixel * WIN + SPAN)
            phase_ref[half, rows, :] = phase_ref[half, rows, :] - base

    @pl.when(owned < OWNERS)
    def _():
        for_peers(lambda other: plane_copy(owned, other).wait_send())

    @pl.when((owned < OWNERS) & (tile == middle))
    def _():
        for_column(lambda other: column_copy(owned, other).wait_send())


def pair_phases(slc, dates, tiles):
    return pl.pallas_call(
        front_kernel,
        out_shape=jax.ShapeDtypeStruct((2, 256, LANES), F32),
        in_specs=[pl.BlockSpec(memory_space=pl.ANY)],
        out_specs=pl.BlockSpec(memory_space=pltpu.VMEM),
        scratch_shapes=[
            pltpu.VMEM(slc.shape, slc.dtype),
            pltpu.VMEM((dates, 8, 16, LANES), jnp.bfloat16),
            pltpu.VMEM((dates, 8, 16, LANES), jnp.bfloat16),
            pltpu.VMEM((8, 2, 256, 256), F32),
            pltpu.VMEM((2, 256, 256), F32),
            pltpu.VMEM((2, 2, 256, LANES), F32),
            pltpu.VMEM((OWNERS, 8, LANES), F32),
            pltpu.VMEM((dates, 8, LANES), F32),
            pltpu.VMEM((OWNERS, 4, LANES), F32),
            pltpu.SemaphoreType.DMA(()),
            pltpu.SemaphoreType.DMA((dates,)),
            pltpu.SemaphoreType.DMA((dates,)),
            pltpu.SemaphoreType.DMA((OWNERS,)),
            pltpu.SemaphoreType.DMA((dates,)),
            pltpu.SemaphoreType.DMA((tiles,)),
            pltpu.SemaphoreType.DMA((1,)),
            pltpu.SemaphoreType.DMA((dates,)),
            pltpu.SemaphoreType.DMA((OWNERS,)),
        ],
        compiler_params=pltpu.CompilerParams(collective_id=0, has_side_effects=True),
        name="pair_phases",
    )(slc)


def aligned(value, unit):
    return value if isinstance(value, int) else pl.multiple_of(value, unit)


def factor_step(block, mat_ref, rhs_ref, low_ref, back_ref, sol_ref, tiles=3):
    base = aligned(block * 256, 256)

    def spread(ref, row):
        return jnp.broadcast_to(ref[pl.ds(row, 1), :], (8, LANES))

    s = {}
    for i in range(8):
        for j in range(i, 8):
            s[i, j] = spread(mat_ref, base + i * WIN + j)
    rows = []
    for i in range(8):
        later = [mat_ref[pl.ds(aligned(base + i * WIN + 8 * t, 8), 8), :] for t in range(1, tiles + 1)]
        rows.append(later + [spread(rhs_ref, block * 8 + i)])
    mult = {}
    inverse = []
    for a in (0, 2, 4, 6):
        b = a + 1
        det = s[a, a] * s[b, b] - s[a, b] * s[a, b]
        scale = 1.0 / det
        e11, e12, e22 = s[b, b] * scale, -s[a, b] * scale, s[a, a] * scale
        inverse.append((e11, e12, e22))
        for i in range(a + 2, 8):
            mult[i, a] = s[a, i] * e11 + s[b, i] * e12
            mult[i, b] = s[a, i] * e12 + s[b, i] * e22
        for i in range(a + 2, 8):
            for j in range(i, 8):
                s[i, j] = s[i, j] - mult[i, a] * s[a, j] - mult[i, b] * s[b, j]
        for i in range(a + 2, 8):
            rows[i] = [rows[i][t] - mult[i, a] * rows[a][t] - mult[i, b] * rows[b][t] for t in range(tiles + 1)]
    scaled = [None] * 8
    for index, a in enumerate((0, 2, 4, 6)):
        e11, e12, e22 = inverse[index]
        scaled[a] = [e11 * rows[a][t] + e12 * rows[a + 1][t] for t in range(tiles + 1)]
        scaled[a + 1] = [e12 * rows[a][t] + e22 * rows[a + 1][t] for t in range(tiles + 1)]
    for k in range(8):
        for t in range(tiles):
            low_ref[k * 24 + 8 * t:k * 24 + 8 * t + 8, :] = scaled[k][t]
    for r in range(8 * tiles):
        t = r // 8
        target = aligned((block + 1) * 256, 256) + r * WIN
        first = max(r - 16, 0) // 2 * 2
        factors = {k: jnp.broadcast_to(low_ref[k * 24 + r:k * 24 + r + 1, :], (8, LANES))
                   for k in range(first, 8)}
        for u in range(t, tiles):
            where = pl.ds(aligned(target + (u - t) * 8, 8), 8)
            value = mat_ref[where, :]
            for k in range(first, 8):
                value = value - factors[k] * rows[k][u]
            mat_ref[where, :] = value
    for u in range(tiles):
        where = pl.ds(aligned((block + 1 + u) * 8, 8), 8)
        value = rhs_ref[where, :]
        for k in range(8):
            value = value - scaled[k][tiles] * rows[k][u]
        rhs_ref[where, :] = value
    for a in (6, 4, 2, 0):
        for c in (a, a + 1):
            for i in range(a + 2, 8):
                scaled[c] = [scaled[c][t] - mult[i, c] * scaled[i][t] for t in range(tiles + 1)]
    sub = lax.broadcasted_iota(jnp.int32, (8, LANES), 0)
    answer = scaled[0][tiles]
    for i in range(1, 8):
        answer = jnp.where(sub == i, scaled[i][tiles], answer)
    sol_ref[pl.ds(aligned(block * 8, 8), 8), :] = answer
    for i in range(8):
        for t in range(tiles):
            back_ref[pl.ds((block * 24 + 8 * t) * 9 + i, 8, stride=9), :] = scaled[i][t]


def tree_sum(parts):
    while len(parts) > 1:
        parts = [parts[i] + parts[i + 1] if i + 1 < len(parts) else parts[i]
                 for i in range(0, len(parts), 2)]
    return parts[0]


def back_step(block, back_ref, sol_ref, tiles=3):
    rows = slice(block * 8, block * 8 + 8)

    def product(c):
        start = (block * 24 + c) * 9
        later = jnp.broadcast_to(sol_ref[block * 8 + 8 + c:block * 8 + 9 + c, :], (8, LANES))
        return back_ref[pl.ds(start, 8), :] * later

    value = sol_ref[rows, :]
    if tiles > 1:
        value = value - tree_sum([product(c) for c in range(8, 8 * tiles)])
    if tiles > 0:
        sol_ref[rows, :] = value - tree_sum([product(c) for c in range(8)])


ENDS = 14
LAST = 17


def join_ends(mat_ref, rhs_ref, tmp_ref):
    mine = lax.broadcasted_iota(jnp.int32, (8, LANES), 1) < 8
    for first in range(ENDS, LAST):
        for second in range(first, LAST):
            u = second - first
            for row in range(8):
                start = (first * 8 + row) * WIN + 8 * u
                value = jnp.where(mine, pltpu.roll(mat_ref[start:start + 8, :], LANES - 8, 1), 0.0)
                tmp_ref[pl.ds(7 - row, 8, stride=9), :] = value
            for row in range(8):
                start = ((31 - second) * 8 + row) * WIN + 8 * u
                mat_ref[start:start + 8, :] = mat_ref[start:start + 8, :] + tmp_ref[pl.ds((7 - row) * 9, 8), :]
        value = jnp.where(mine, pltpu.roll(rhs_ref[first * 8:first * 8 + 8, :], LANES - 8, 1), 0.0)
        for row in range(8):
            tmp_ref[80 + 7 - row:80 + 8 - row, :] = value[row:row + 1]
        start = (31 - first) * 8
        rhs_ref[start:start + 8, :] = rhs_ref[start:start + 8, :] + tmp_ref[80:88, :]


def spread_middle(sol_ref, tmp_ref):
    lane = lax.broadcasted_iota(jnp.int32, (8, LANES), 1)
    for block in range(ENDS, LAST + 1):
        value = pltpu.roll(sol_ref[block * 8:block * 8 + 8, :], 8, 1)
        for row in range(8):
            where = (LAST - block) * 8 + 7 - row
            tmp_ref[where:where + 1, :] = value[row:row + 1]
    for block in range(ENDS, LAST + 1):
        other = tmp_ref[(block - ENDS) * 8:(block - ENDS) * 8 + 8, :]
        rows = slice(block * 8, block * 8 + 8)
        sol_ref[rows, :] = jnp.where(lane < 8, sol_ref[rows, :], other)


def solve_kernel(phase_ref, offset_ref, out_ref, live_ref, mat_ref, rhs_ref, low_ref, back_ref, sol_ref, tmp_ref):
    lane = lax.broadcasted_iota(jnp.int32, (8, LANES), 1)
    backwards = LANES - 1 - lane

    def flipped(value):
        return jnp.take_along_axis(value, backwards, axis=1, mode="promise_in_bounds")

    distance = SPAN - lax.broadcasted_iota(jnp.int32, (SPAN, LANES), 0)
    for h in range(2):
        hit = jnp.zeros((SPAN, LANES), F32)
        for k in range(offset_ref.shape[0]):
            entry = jnp.broadcast_to(offset_ref[k:k + 1, h * LANES:(h + 1) * LANES], (SPAN, LANES))
            hit = jnp.where(entry == distance, 1.0, hit)
        live_ref[h] = hit
    sol_ref[...] = jnp.zeros_like(sol_ref)
    blank = jnp.zeros((8, LANES), F32)

    def turned(pairs):
        rows = []
        for low, high in pairs:
            rows += [low, flipped(high)]
        rows += [blank] * (16 - len(rows))
        return jnp.concatenate(rows, axis=0).T

    def current():
        value = sol_ref[0:LANES, :].T
        return [value[:8], flipped(value[8:16])]

    def ahead(pair, shift):
        a, b = (pltpu.roll(v, LANES - shift, 1) for v in pair)
        keep = lane < LANES - shift
        return [jnp.where(keep, a, b), jnp.where(keep, b, a)]

    def behind(pair, shift):
        a, b = (pltpu.roll(v, shift, 1) for v in pair)
        keep = lane >= shift
        return [jnp.where(keep, a, b), jnp.where(keep, b, a)]

    def one_round(first):
        now = [blank, blank] if first else current()
        degree = [jnp.full((8, LANES), ridge_weight, F32) for _ in range(2)]
        right = [jnp.zeros((8, LANES), F32) for _ in range(2)]
        zero = jnp.zeros((8, LANES), F32)
        for row in range(LANES):
            mat_ref[row * WIN + 24:row * WIN + 32, :] = zero
        for row in range(LANES, 144):
            for t in range(4):
                mat_ref[row * WIN + 8 * t:row * WIN + 8 * t + 8, :] = zero
        rhs_ref[128:136, :] = zero
        rhs_ref[136:144, :] = zero

        stack = []
        for d in range(1, SPAN + 1):
            later = now if first else ahead(now, d)
            weights, moments = [], []
            for h in range(2):
                phase = phase_ref[h, pl.ds(SPAN - d, 8, stride=WIN), :]
                residual = phase if first else phase - (now[h] - later[h])
                live = jnp.broadcast_to(live_ref[h, SPAN - d:SPAN - d + 1, :], (8, LANES))
                weight = live / jnp.maximum(jnp.abs(residual), floor_value)
                weights.append(weight)
                moments.append(weight * phase)
            from_w, from_m = behind(weights, d), behind(moments, d)
            for h in range(2):
                degree[h] = degree[h] + (weights[h] + from_w[h])
                right[h] = right[h] + (moments[h] - from_m[h])
            crossing = jnp.where(lane < min(d, 16), 0.0, from_w[1])
            stack.append((-weights[0], -crossing))
            if len(stack) == 8:
                columns = turned(stack)
                for e in range(8):
                    column = columns if e == 0 else pltpu.roll(columns, LANES - 16 * e, 1)
                    for b in range(16):
                        where = pl.ds(b * 256 + d - 7 + e, 8, stride=WIN + 1)
                        mat_ref[where, :] = column[b * 8:b * 8 + 8]
                stack = []
        columns = turned([degree, right])
        for b in range(16):
            mat_ref[pl.ds(b * 256, 8, stride=WIN + 1), :] = columns[b * 8:b * 8 + 8]
        rhs_ref[0:LANES, :] = pltpu.roll(columns, LANES - 16, 1)

        def forward(i, c):
            factor_step(i, mat_ref, rhs_ref, low_ref, back_ref, sol_ref)
            return c

        lax.fori_loop(0, ENDS, forward, 0, unroll=2)
        join_ends(mat_ref, rhs_ref, tmp_ref)
        for block in range(ENDS, LAST + 1):
            factor_step(block, mat_ref, rhs_ref, low_ref, back_ref, sol_ref, LAST - block)

        for block in range(LAST, ENDS - 1, -1):
            back_step(block, back_ref, sol_ref, LAST - block)
        spread_middle(sol_ref, tmp_ref)
        for block in range(ENDS - 1, -1, -1):
            back_step(block, back_ref, sol_ref)

    for number in range(ITERS):
        one_round(number == 0)
    now = current()
    for h in range(2):
        out_ref[:, h * LANES:(h + 1) * LANES] = now[h]


def solve(phases, offsets):
    return pl.pallas_call(
        solve_kernel,
        out_shape=jax.ShapeDtypeStruct((8, 256), F32),
        in_specs=[pl.BlockSpec(memory_space=pltpu.VMEM)] * 2,
        out_specs=pl.BlockSpec(memory_space=pltpu.VMEM),
        scratch_shapes=[
            pltpu.VMEM((2, SPAN, LANES), F32),
            pltpu.VMEM((168 * WIN, LANES), F32),
            pltpu.VMEM((168, LANES), F32),
            pltpu.VMEM((8 * 24, LANES), F32),
            pltpu.VMEM((18 * 24 * 9, LANES), F32),
            pltpu.VMEM((168, LANES), F32),
            pltpu.VMEM((96, LANES), F32),
        ],
        name="solve",
    )(phases, offsets)


def local(slc, offsets):
    rows_first = jnp.transpose(slc, (0, 2, 1, 3))
    phases = pair_phases(rows_first, lax.axis_size("date"), lax.axis_size("tile"))
    series = solve(phases, offsets.T)
    return series.T[:, None, :]


def solution(mesh):
    return jax.shard_map(
        local,
        mesh=mesh,
        in_specs=(P(None, "date", None, "tile"), P()),
        out_specs=P(None, "tile", "date"),
        check_vma=False,
    )
```

```python
import jax
import jax.numpy as jnp
from jax import lax
from jax.experimental import pallas as pl
from jax.experimental.pallas import tpu as pltpu
from jax.sharding import PartitionSpec as P

LOOK_AZ = 5
LOOK_RG = 20
SPAN = 24
ITERS = 2
LANES = 128
WIN = 32

floor_value = 0.05
ridge_weight = 1.0
F32 = jnp.float32
MESH = pl.DeviceIdType.MESH
OWNERS = 12
OWNER_STEP = 5
OWNER_INVERSE = 13
RING = 4


def gather_step(step, slc_ref, send_ref):
    lane = lax.broadcasted_iota(jnp.int32, (16, LANES), 1)
    half = step // 4
    quarter = step % 4
    blank = jnp.zeros((16, LANES), F32)
    moved = []
    for rho in range(LOOK_AZ):
        amount = LOOK_RG * rho
        line = []
        for t in range(5):
            columns = pl.ds(pl.multiple_of((quarter * 5 + t) * LANES, LANES), LANES)
            row = half * LOOK_AZ + rho
            line.append(jnp.concatenate([
                slc_ref[0, row, :, columns].astype(F32),
                slc_ref[1, row, :, columns].astype(F32),
            ], axis=0))
        if amount == 0:
            moved.append(line + [blank])
            continue
        rolled = [blank] + [pltpu.roll(v, amount, 1) for v in line] + [blank]
        moved.append([jnp.where(lane < amount, rolled[t], rolled[t + 1]) for t in range(6)])
    for local_pixel in range(32):
        start = LOOK_RG * local_pixel
        tile, offset = start // LANES, start % LANES
        out = blank
        for rho in range(LOOK_AZ):
            lo = offset + LOOK_RG * rho
            hi = lo + LOOK_RG
            if lo < LANES:
                out = jnp.where((lane >= lo) & (lane < hi), moved[rho][tile], out)
            if hi > LANES:
                mask = (lane >= lo - LANES) & (lane < hi - LANES)
                out = jnp.where(mask, moved[rho][tile + 1], out)
        slot = half * 16 + quarter * 4 + local_pixel // 8
        send_ref[slot, local_pixel % 8] = out.astype(jnp.bfloat16)


def skewed(gram_ref, index, block, place):
    rows = pl.ds(block * 8, 8)
    first = gram_ref[index + (rows, pl.ds(0, LANES))] if block >= 13 else None
    second = gram_ref[index + (rows, pl.ds(LANES, LANES))] if block < 16 else None
    if first is None:
        value = second
    elif second is None:
        value = first
    else:
        lane = lax.broadcasted_iota(jnp.int32, (8, LANES), 1)
        value = jnp.where(lane >= 64, first, second)
    shift = (place * WIN + SPAN + 1 + block * 8) % LANES
    return pltpu.roll(value, shift, 1, stride=1, stride_axis=0)


def front_kernel(slc_hbm, phase_ref, slc_ref, send_ref, recv_ref, gram_ref, total_ref, band_ref,
                 part_ref, gathered_ref, anchor_ref, load_sem, send_sem, recv_sem, part_send,
                 part_recv, column_send, column_recv, plane_send, plane_recv):
    dates = send_ref.shape[0]
    tiles = lax.axis_size("tile")
    me = lax.axis_index("date")
    tile = lax.axis_index("tile")
    middle = tiles // 2
    lane = lax.broadcasted_iota(jnp.int32, (8, LANES), 1)
    load = pltpu.make_async_copy(slc_hbm, slc_ref, load_sem)
    load.start()

    def peer(k):
        return me ^ (dates - 1 - k)

    def for_peers(action):
        def go(k, carry):
            action(peer(k))
            return carry

        lax.fori_loop(0, dates - 1, go, 0, unroll=True)

    def for_far_peers(action):
        steps = [(dx, dy, dc) for dx in range(RING) for dy in range(RING) for dc in range(2)]
        steps.sort(key=lambda v: -(min(v[0], RING - v[0]) + min(v[1], RING - v[1]) + v[2] / 4))
        for dx, dy, dc in steps[:-1]:
            across = (me // (2 * RING) + dx) % RING
            along = (me // 2 + dy) % RING
            core = (me + dc) % 2
            action((across * RING + along) * 2 + core)

    def for_column(action):
        def go(k, carry):
            action(lax.rem(tile + k, tiles))
            return carry

        lax.fori_loop(1, tiles, go, 0)

    barrier = pltpu.get_barrier_semaphore()
    for_column(lambda other: pl.semaphore_signal(
        barrier, inc=1, device_id={"tile": other}, device_id_type=MESH))
    for_peers(lambda other: pl.semaphore_signal(
        barrier, inc=1, device_id={"date": other}, device_id_type=MESH))
    load.wait()

    def sample_copy(other, slot):
        return pltpu.make_async_remote_copy(
            src_ref=send_ref.at[other], dst_ref=recv_ref.at[slot],
            send_sem=send_sem.at[other], recv_sem=recv_sem.at[slot],
            device_id={"date": other}, device_id_type=MESH)

    def gather(step, carry):
        gather_step(step, slc_ref, send_ref)
        return carry

    lax.fori_loop(0, 8, gather, 0, unroll=2)
    pl.semaphore_wait(barrier, dates - 1 + tiles - 1)
    for_far_peers(lambda other: sample_copy(other, me).start())
    recv_ref[me] = send_ref[me]

    row_id = lax.broadcasted_iota(jnp.int32, (256, 256), 0)
    col_id = lax.broadcasted_iota(jnp.int32, (256, 256), 1)
    mirror = (row_id + col_id == 255).astype(F32).astype(jnp.bfloat16)
    contract = (((1,), (1,)), ((), ()))

    for_peers(lambda other: sample_copy(other, other).wait_recv())
    for pixel in range(8):
        both = recv_ref[:, pixel].astype(F32)
        real = both[:, :8].reshape(256, LANES)
        imag = both[:, 8:].reshape(256, LANES)
        right = jnp.concatenate([real, imag], axis=1).astype(jnp.bfloat16)
        turned = jnp.concatenate([imag, -real], axis=1).astype(jnp.bfloat16)
        descending = jnp.dot(mirror, right, preferred_element_type=F32).astype(jnp.bfloat16)
        for part, left in enumerate((right, turned)):
            gram = lax.dot_general(left, descending, contract, preferred_element_type=F32)
            gram_ref[pixel, part] = gram
            if pixel == 0:
                total_ref[part] = gram
            else:
                total_ref[part] = total_ref[part] + gram

    def owner_date(owner):
        return lax.rem(owner * OWNER_STEP, dates)

    owned = lax.rem(me * OWNER_INVERSE, dates)

    def part_copy(owner, slot):
        return pltpu.make_async_remote_copy(
            src_ref=part_ref.at[owner], dst_ref=gathered_ref.at[slot],
            send_sem=part_send.at[owner], recv_sem=part_recv.at[slot],
            device_id={"date": owner_date(owner)}, device_id_type=MESH)

    def for_owners(action):
        def go(owner, carry):
            @pl.when(owner != owned)
            def _():
                action(owner)

            return carry

        lax.fori_loop(0, OWNERS, go, 0, unroll=True)

    @pl.when(tile == middle)
    def _():
        for block in range(32):
            value = jnp.where(lane < WIN, skewed(total_ref, (0,), block, 0), skewed(total_ref, (1,), block, 1))
            band_ref[0, 0, block * 8:block * 8 + 8, :] = value
        for half in range(2):
            turned = band_ref[0, 0, half * LANES:(half + 1) * LANES, :].T
            for sixth in range(6):
                owner = half * 6 + sixth
                part_ref[owner, 0:4, :] = turned[sixth * 4:sixth * 4 + 4]
                part_ref[owner, 4:8, :] = turned[WIN + sixth * 4:WIN + sixth * 4 + 4]
        for_owners(lambda owner: part_copy(owner, me).start())

    def bands(group, carry):
        for part in range(2):
            for block in range(32):
                value = skewed(gram_ref, (group * 4, part), block, 0)
                for place in range(1, 4):
                    other = skewed(gram_ref, (group * 4 + place, part), block, place)
                    value = jnp.where(lane < place * WIN, value, other)
                band_ref[part, group, block * 8:block * 8 + 8, :] = value
        for half in range(2):
            rows = slice(half * LANES, (half + 1) * LANES)
            real = band_ref[0, group, rows, :].T
            imag = band_ref[1, group, rows, :].T
            phase_ref[half, pl.ds(pl.multiple_of(group * LANES, LANES), LANES), :] = jnp.arctan2(imag, real)
        return carry

    lax.fori_loop(0, 2, bands, 0)

    def column_copy(owner, other):
        return pltpu.make_async_remote_copy(
            src_ref=anchor_ref.at[owner], dst_ref=anchor_ref.at[owner],
            send_sem=column_send.at[other], recv_sem=column_recv.at[0],
            device_id={"tile": other}, device_id_type=MESH)

    def plane_copy(owner, other):
        return pltpu.make_async_remote_copy(
            src_ref=anchor_ref.at[owner], dst_ref=anchor_ref.at[owner],
            send_sem=plane_send.at[other], recv_sem=plane_recv.at[owner],
            device_id={"date": other}, device_id_type=MESH)

    @pl.when((owned < OWNERS) & (tile == middle))
    def _():
        def part_arrive(k, total):
            other = peer(k)
            part_copy(owned, other).wait_recv()
            return total + gathered_ref[other]

        total = lax.fori_loop(0, dates - 1, part_arrive, part_ref[owned])
        anchor_ref[owned] = jnp.arctan2(total[4:], total[:4])
        for_column(lambda other: column_copy(owned, other).start())

    @pl.when((owned < OWNERS) & (tile != middle))
    def _():
        column_copy(owned, middle).wait_recv()

    @pl.when(owned < OWNERS)
    def _():
        for_far_peers(lambda other: plane_copy(owned, other).start())

    for_peers(lambda other: sample_copy(other, me).wait_send())

    @pl.when(tile == middle)
    def _():
        for_owners(lambda owner: part_copy(owner, me).wait_send())

    for_owners(lambda owner: plane_copy(owner, owner_date(owner)).wait_recv())

    for half in range(2):
        base = jnp.concatenate([anchor_ref[half * 6 + t] for t in range(6)], axis=0)
        for pixel in range(8):
            rows = slice(pixel * WIN, pixel * WIN + SPAN)
            phase_ref[half, rows, :] = phase_ref[half, rows, :] - base

    @pl.when(owned < OWNERS)
    def _():
        for_peers(lambda other: plane_copy(owned, other).wait_send())

    @pl.when((owned < OWNERS) & (tile == middle))
    def _():
        for_column(lambda other: column_copy(owned, other).wait_send())


def pair_phases(slc, dates, tiles):
    return pl.pallas_call(
        front_kernel,
        out_shape=jax.ShapeDtypeStruct((2, 256, LANES), F32),
        in_specs=[pl.BlockSpec(memory_space=pl.ANY)],
        out_specs=pl.BlockSpec(memory_space=pltpu.VMEM),
        scratch_shapes=[
            pltpu.VMEM(slc.shape, slc.dtype),
            pltpu.VMEM((dates, 8, 16, LANES), jnp.bfloat16),
            pltpu.VMEM((dates, 8, 16, LANES), jnp.bfloat16),
            pltpu.VMEM((8, 2, 256, 256), F32),
            pltpu.VMEM((2, 256, 256), F32),
            pltpu.VMEM((2, 2, 256, LANES), F32),
            pltpu.VMEM((OWNERS, 8, LANES), F32),
            pltpu.VMEM((dates, 8, LANES), F32),
            pltpu.VMEM((OWNERS, 4, LANES), F32),
            pltpu.SemaphoreType.DMA(()),
            pltpu.SemaphoreType.DMA((dates,)),
            pltpu.SemaphoreType.DMA((dates,)),
            pltpu.SemaphoreType.DMA((OWNERS,)),
            pltpu.SemaphoreType.DMA((dates,)),
            pltpu.SemaphoreType.DMA((tiles,)),
            pltpu.SemaphoreType.DMA((1,)),
            pltpu.SemaphoreType.DMA((dates,)),
            pltpu.SemaphoreType.DMA((OWNERS,)),
        ],
        compiler_params=pltpu.CompilerParams(collective_id=0, has_side_effects=True),
        name="pair_phases",
    )(slc)


def aligned(value, unit):
    return value if isinstance(value, int) else pl.multiple_of(value, unit)


def factor_step(block, mat_ref, rhs_ref, low_ref, back_ref, sol_ref, tiles=3):
    base = aligned(block * 256, 256)

    def spread(ref, row):
        return jnp.broadcast_to(ref[pl.ds(row, 1), :], (8, LANES))

    s = {}
    for i in range(8):
        for j in range(i, 8):
            s[i, j] = spread(mat_ref, base + i * WIN + j)
    rows = []
    for i in range(8):
        later = [mat_ref[pl.ds(aligned(base + i * WIN + 8 * t, 8), 8), :] for t in range(1, tiles + 1)]
        rows.append(later + [spread(rhs_ref, block * 8 + i)])
    mult = {}
    inverse = []
    for a in (0, 2, 4, 6):
        b = a + 1
        det = s[a, a] * s[b, b] - s[a, b] * s[a, b]
        scale = 1.0 / det
        e11, e12, e22 = s[b, b] * scale, -s[a, b] * scale, s[a, a] * scale
        inverse.append((e11, e12, e22))
        for i in range(a + 2, 8):
            mult[i, a] = s[a, i] * e11 + s[b, i] * e12
            mult[i, b] = s[a, i] * e12 + s[b, i] * e22
        for i in range(a + 2, 8):
            for j in range(i, 8):
                s[i, j] = s[i, j] - mult[i, a] * s[a, j] - mult[i, b] * s[b, j]
        for i in range(a + 2, 8):
            rows[i] = [rows[i][t] - mult[i, a] * rows[a][t] - mult[i, b] * rows[b][t] for t in range(tiles + 1)]
    scaled = [None] * 8
    for index, a in enumerate((0, 2, 4, 6)):
        e11, e12, e22 = inverse[index]
        scaled[a] = [e11 * rows[a][t] + e12 * rows[a + 1][t] for t in range(tiles + 1)]
        scaled[a + 1] = [e12 * rows[a][t] + e22 * rows[a + 1][t] for t in range(tiles + 1)]
    for k in range(8):
        for t in range(tiles):
            low_ref[k * 24 + 8 * t:k * 24 + 8 * t + 8, :] = scaled[k][t]
    for r in range(8 * tiles):
        t = r // 8
        target = aligned((block + 1) * 256, 256) + r * WIN
        first = max(r - 16, 0) // 2 * 2
        factors = {k: jnp.broadcast_to(low_ref[k * 24 + r:k * 24 + r + 1, :], (8, LANES))
                   for k in range(first, 8)}
        for u in range(t, tiles):
            where = pl.ds(aligned(target + (u - t) * 8, 8), 8)
            value = mat_ref[where, :]
            for k in range(first, 8):
                value = value - factors[k] * rows[k][u]
            mat_ref[where, :] = value
    for u in range(tiles):
        where = pl.ds(aligned((block + 1 + u) * 8, 8), 8)
        value = rhs_ref[where, :]
        for k in range(8):
            value = value - scaled[k][tiles] * rows[k][u]
        rhs_ref[where, :] = value
    for a in (6, 4, 2, 0):
        for c in (a, a + 1):
            for i in range(a + 2, 8):
                scaled[c] = [scaled[c][t] - mult[i, c] * scaled[i][t] for t in range(tiles + 1)]
    sub = lax.broadcasted_iota(jnp.int32, (8, LANES), 0)
    answer = scaled[0][tiles]
    for i in range(1, 8):
        answer = jnp.where(sub == i, scaled[i][tiles], answer)
    sol_ref[pl.ds(aligned(block * 8, 8), 8), :] = answer
    for i in range(8):
        for t in range(tiles):
            back_ref[pl.ds((block * 24 + 8 * t) * 9 + i, 8, stride=9), :] = scaled[i][t]


def tree_sum(parts):
    while len(parts) > 1:
        parts = [parts[i] + parts[i + 1] if i + 1 < len(parts) else parts[i]
                 for i in range(0, len(parts), 2)]
    return parts[0]


def back_step(block, back_ref, sol_ref, tiles=3):
    rows = slice(block * 8, block * 8 + 8)

    def product(c):
        start = (block * 24 + c) * 9
        later = jnp.broadcast_to(sol_ref[block * 8 + 8 + c:block * 8 + 9 + c, :], (8, LANES))
        return back_ref[pl.ds(start, 8), :] * later

    value = sol_ref[rows, :]
    if tiles > 1:
        value = value - tree_sum([product(c) for c in range(8, 8 * tiles)])
    if tiles > 0:
        sol_ref[rows, :] = value - tree_sum([product(c) for c in range(8)])


ENDS = 14
LAST = 17


def join_ends(mat_ref, rhs_ref, tmp_ref):
    mine = lax.broadcasted_iota(jnp.int32, (8, LANES), 1) < 8
    for first in range(ENDS, LAST):
        for second in range(first, LAST):
            u = second - first
            for row in range(8):
                start = (first * 8 + row) * WIN + 8 * u
                value = jnp.where(mine, pltpu.roll(mat_ref[start:start + 8, :], LANES - 8, 1), 0.0)
                tmp_ref[pl.ds(7 - row, 8, stride=9), :] = value
            for row in range(8):
                start = ((31 - second) * 8 + row) * WIN + 8 * u
                mat_ref[start:start + 8, :] = mat_ref[start:start + 8, :] + tmp_ref[pl.ds((7 - row) * 9, 8), :]
        value = jnp.where(mine, pltpu.roll(rhs_ref[first * 8:first * 8 + 8, :], LANES - 8, 1), 0.0)
        for row in range(8):
            tmp_ref[80 + 7 - row:80 + 8 - row, :] = value[row:row + 1]
        start = (31 - first) * 8
        rhs_ref[start:start + 8, :] = rhs_ref[start:start + 8, :] + tmp_ref[80:88, :]


def spread_middle(sol_ref, tmp_ref):
    lane = lax.broadcasted_iota(jnp.int32, (8, LANES), 1)
    for block in range(ENDS, LAST + 1):
        value = pltpu.roll(sol_ref[block * 8:block * 8 + 8, :], 8, 1)
        for row in range(8):
            where = (LAST - block) * 8 + 7 - row
            tmp_ref[where:where + 1, :] = value[row:row + 1]
    for block in range(ENDS, LAST + 1):
        other = tmp_ref[(block - ENDS) * 8:(block - ENDS) * 8 + 8, :]
        rows = slice(block * 8, block * 8 + 8)
        sol_ref[rows, :] = jnp.where(lane < 8, sol_ref[rows, :], other)


def solve_kernel(phase_ref, offset_ref, out_ref, live_ref, mat_ref, rhs_ref, low_ref, back_ref, sol_ref, tmp_ref):
    lane = lax.broadcasted_iota(jnp.int32, (8, LANES), 1)
    backwards = LANES - 1 - lane

    def flipped(value):
        return jnp.take_along_axis(value, backwards, axis=1, mode="promise_in_bounds")

    distance = SPAN - lax.broadcasted_iota(jnp.int32, (SPAN, LANES), 0)
    for h in range(2):
        hit = jnp.zeros((SPAN, LANES), F32)
        for k in range(offset_ref.shape[0]):
            entry = jnp.broadcast_to(offset_ref[k:k + 1, h * LANES:(h + 1) * LANES], (SPAN, LANES))
            hit = jnp.where(entry == distance, 1.0, hit)
        live_ref[h] = hit
    sol_ref[...] = jnp.zeros_like(sol_ref)
    blank = jnp.zeros((8, LANES), F32)

    def turned(pairs):
        rows = []
        for low, high in pairs:
            rows += [low, flipped(high)]
        rows += [blank] * (16 - len(rows))
        return jnp.concatenate(rows, axis=0).T

    def current():
        value = sol_ref[0:LANES, :].T
        return [value[:8], flipped(value[8:16])]

    def ahead(pair, shift):
        a, b = (pltpu.roll(v, LANES - shift, 1) for v in pair)
        keep = lane < LANES - shift
        return [jnp.where(keep, a, b), jnp.where(keep, b, a)]

    def behind(pair, shift):
        a, b = (pltpu.roll(v, shift, 1) for v in pair)
        keep = lane >= shift
        return [jnp.where(keep, a, b), jnp.where(keep, b, a)]

    def one_round(first):
        now = [blank, blank] if first else current()
        degree = [jnp.full((8, LANES), ridge_weight, F32) for _ in range(2)]
        right = [jnp.zeros((8, LANES), F32) for _ in range(2)]
        zero = jnp.zeros((8, LANES), F32)
        for row in range(LANES):
            mat_ref[row * WIN + 24:row * WIN + 32, :] = zero
        for row in range(LANES, 144):
            for t in range(4):
                mat_ref[row * WIN + 8 * t:row * WIN + 8 * t + 8, :] = zero
        rhs_ref[128:136, :] = zero
        rhs_ref[136:144, :] = zero

        stack = []
        for d in range(1, SPAN + 1):
            later = now if first else ahead(now, d)
            weights, moments = [], []
            for h in range(2):
                phase = phase_ref[h, pl.ds(SPAN - d, 8, stride=WIN), :]
                residual = phase if first else phase - (now[h] - later[h])
                live = jnp.broadcast_to(live_ref[h, SPAN - d:SPAN - d + 1, :], (8, LANES))
                weight = live / jnp.maximum(jnp.abs(residual), floor_value)
                weights.append(weight)
                moments.append(weight * phase)
            from_w, from_m = behind(weights, d), behind(moments, d)
            for h in range(2):
                degree[h] = degree[h] + (weights[h] + from_w[h])
                right[h] = right[h] + (moments[h] - from_m[h])
            crossing = jnp.where(lane < min(d, 16), 0.0, from_w[1])
            stack.append((-weights[0], -crossing))
            if len(stack) == 8:
                columns = turned(stack)
                for e in range(8):
                    column = columns if e == 0 else pltpu.roll(columns, LANES - 16 * e, 1)
                    for b in range(16):
                        where = pl.ds(b * 256 + d - 7 + e, 8, stride=WIN + 1)
                        mat_ref[where, :] = column[b * 8:b * 8 + 8]
                stack = []
        columns = turned([degree, right])
        for b in range(16):
            mat_ref[pl.ds(b * 256, 8, stride=WIN + 1), :] = columns[b * 8:b * 8 + 8]
        rhs_ref[0:LANES, :] = pltpu.roll(columns, LANES - 16, 1)

        def forward(i, c):
            factor_step(i, mat_ref, rhs_ref, low_ref, back_ref, sol_ref)
            return c

        lax.fori_loop(0, ENDS, forward, 0, unroll=2)
        join_ends(mat_ref, rhs_ref, tmp_ref)
        for block in range(ENDS, LAST + 1):
            factor_step(block, mat_ref, rhs_ref, low_ref, back_ref, sol_ref, LAST - block)

        for block in range(LAST, ENDS - 1, -1):
            back_step(block, back_ref, sol_ref, LAST - block)
        spread_middle(sol_ref, tmp_ref)
        for block in range(ENDS - 1, -1, -1):
            back_step(block, back_ref, sol_ref)

    for number in range(ITERS):
        one_round(number == 0)
    now = current()
    for h in range(2):
        out_ref[:, h * LANES:(h + 1) * LANES] = now[h]


def solve(phases, offsets):
    return pl.pallas_call(
        solve_kernel,
        out_shape=jax.ShapeDtypeStruct((8, 256), F32),
        in_specs=[pl.BlockSpec(memory_space=pltpu.VMEM)] * 2,
        out_specs=pl.BlockSpec(memory_space=pltpu.VMEM),
        scratch_shapes=[
            pltpu.VMEM((2, SPAN, LANES), F32),
            pltpu.VMEM((168 * WIN, LANES), F32),
            pltpu.VMEM((168, LANES), F32),
            pltpu.VMEM((8 * 24, LANES), F32),
            pltpu.VMEM((18 * 24 * 9, LANES), F32),
            pltpu.VMEM((168, LANES), F32),
            pltpu.VMEM((96, LANES), F32),
        ],
        name="solve",
    )(phases, offsets)


def local(slc, offsets):
    rows_first = jnp.transpose(slc, (0, 2, 1, 3))
    phases = pair_phases(rows_first, lax.axis_size("date"), lax.axis_size("tile"))
    series = solve(phases, offsets.T)
    return series.T[:, None, :]


def solution(mesh):
    return jax.shard_map(
        local,
        mesh=mesh,
        in_specs=(P(None, "date", None, "tile"), P()),
        out_specs=P(None, "tile", "date"),
        check_vma=False,
    )
```
